256 devices in a mesh: tm: 16 (over z_hi, y), gx: 4 (over z_lo, core), gy: 4 (over x).
Axes of the slice: x: 4, y: 4, z: 8 (z_hi: 4, z_lo: 2; z = z_hi * 2 + z_lo), core: 2. Of those that a mesh axis runs over, the one named last changes fastest.
Arguments:
- provisional: float32 [16, 3, 3, 16, 64, 1024], P('tm', None, None, None, 'gx', 'gy'), may hold values from -1.5 to 1.5
Outputs:
- corrected: float32 [16, 3, 3, 16, 64, 1024], P('tm', None, None, None, 'gx', 'gy')
The draws below stay inside these ranges and needn't reach their ends.
All inputs are finite; a program needn't handle non-finite values.
Results may differ from the reference program's by a relative error of at most 0.00002.
Values sent between devices are 32-bit elements; how exact they have to be, the bound alone decides.
No kernel may reach another device: no remote copies, remote signals or barrier semaphores. Data moves between devices by JAX's collectives and lax.ppermute only.
A program may use at most 64 MiB of HBM per device.

```python
import jax
import jax.numpy as jnp

NZ = 16
SLICES = 16
NX = 64
NY = 1024
N_TM = 16


def level_of(key, dims, split, low, high):
    factor_of, own = 1.0, jax.random.fold_in(key, 6)
    for position, blocks in split:
        steps = jnp.exp(jax.random.uniform(jax.random.fold_in(own, position), (blocks,), jnp.float32, low / len(split), high / len(split)))
        factor_of = factor_of * jnp.repeat(steps, dims[position] // blocks).reshape([-1 if axis == position else 1 for axis in range(len(dims))])
    return factor_of


def noise(rng, dims, scale, reach, split=(), kind=jnp.bfloat16):
    drawn = jax.random.normal(rng, dims, jnp.float32) * scale
    if len(split) > 0:
        drawn = level_of(rng, dims, split, -0.22, 0.18) * drawn
    return jnp.clip(drawn, min=-reach, max=reach).astype(kind)


def setup_inputs(seed: int = 0) -> dict:
    splits = jax.random.split(jax.random.key(seed), 2)
    return {
        "provisional": noise(splits[0], (SLICES, 3, 3, NZ, NX, NY), 0.25, 1.5, ((0, 16), (4, 4), (5, 4)), jnp.float32),
    }


viscosity = 0.1
slice_step = 0.25
half_step = 0.125
first_row = (5.0 / 24.0, 1.0 / 3.0, -1.0 / 24.0)
second_row = (-1.0 / 24.0, 1.0 / 3.0, 5.0 / 24.0)


def tendency(padded, spacing):
    centre = padded[:, :, 1:-1, 1:-1]
    east_side = padded[:, :, 2:, 1:-1]
    west_side = padded[:, :, :-2, 1:-1]
    north_side = padded[:, :, 1:-1, 2:]
    south_side = padded[:, :, 1:-1, :-2]
    upper_side = jnp.roll(centre, -1, axis=1)
    lower_side = jnp.roll(centre, 1, axis=1)
    change_first = 0.5 * (east_side - west_side)
    change_second = (0.5 / spacing) * (north_side - south_side)
    change_third = 0.5 * (upper_side - lower_side)
    laplace = (east_side + west_side - 2.0 * centre) + (north_side + south_side - 2.0 * centre) / (spacing * spacing) + (upper_side + lower_side - 2.0 * centre)
    transport = centre[0:1] * change_first + centre[1:2] * change_second + centre[2:3] * change_third
    return viscosity * laplace - transport


def evaluate(field, spacing):
    return tendency(jnp.pad(field, ((0, 0), (0, 0), (1, 1), (1, 1))), spacing)


def quadrature(values, weights):
    return slice_step * (weights[0] * values[0] + weights[1] * values[1] + weights[2] * values[2])


def restrict(field):
    return 0.5 * (field[..., 0::2] + field[..., 1::2])


def prolong(field):
    return jnp.repeat(field, 2, axis=-1)


def reference(provisional):
    outputs = []
    carried_coarse = None
    carried_fine = None
    for slice_index in range(N_TM):
        start_node = provisional[slice_index, 0]
        middle_node = provisional[slice_index, 1]
        final_node = provisional[slice_index, 2]
        old_fluxes = (evaluate(start_node, 1.0), evaluate(middle_node, 1.0), evaluate(final_node, 1.0))
        new_middle = start_node + quadrature(old_fluxes, first_row)
        slope_middle = evaluate(new_middle, 1.0)
        new_final = new_middle + half_step * (slope_middle - old_fluxes[1]) + quadrature(old_fluxes, second_row)
        slope_final = evaluate(new_final, 1.0)
        coarse_start = restrict(start_node)
        coarse_middle = restrict(new_middle)
        coarse_final = restrict(new_final)
        new_fluxes = (old_fluxes[0], slope_middle, slope_final)
        integral_first = restrict(quadrature(new_fluxes, first_row))
        integral_second = restrict(quadrature(new_fluxes, second_row))
        base_start = evaluate(coarse_start, 2.0)
        base_middle = evaluate(coarse_middle, 2.0)
        chain_start = coarse_start if slice_index == 0 else carried_coarse
        chain_middle = chain_start + half_step * (evaluate(chain_start, 2.0) - base_start) + integral_first
        chain_final = chain_middle + half_step * (evaluate(chain_middle, 2.0) - base_middle) + integral_second
        out_middle = new_middle + prolong(chain_middle - coarse_middle)
        out_final = new_final + prolong(chain_final - coarse_final)
        out_start = start_node if slice_index == 0 else carried_fine
        outputs.append(jnp.stack([out_start, out_middle, out_final]))
        carried_coarse = chain_final
        carried_fine = out_final
    return jnp.stack(outputs)
```

```python
import jax
import jax.numpy as jnp
from jax import lax
from jax.experimental import pallas as pl
from jax.experimental.pallas import tpu as pltpu
from jax.sharding import Mesh
from jax.sharding import PartitionSpec as P

viscosity = 0.1
slice_step = 0.25
half_step = 0.125
first_row = (5.0 / 24.0, 1.0 / 3.0, -1.0 / 24.0)
second_row = (-1.0 / 24.0, 1.0 / 3.0, 5.0 / 24.0)

f32 = jnp.float32
highest = lax.Precision.HIGHEST
group_axes = ("ty", "gx")


def lanes(shape):
    return lax.broadcasted_iota(jnp.int32, shape, len(shape) - 1)


def strided(u, k, x, half):
    return u[pl.ds(k * 512 + x // 8 * 16 + half * 8 + x % 8, 16, stride=32), :]


def edges_body(u, low_rows, high_rows, low_columns, high_columns):
    slot = lanes((16, 128)) // 8

    def each(k, carry):
        left = jnp.zeros((16, 128), f32)
        right = jnp.zeros((16, 128), f32)
        for x in range(16):
            a = strided(u, k, x, 0)
            b = strided(u, k, x, 1)
            if x < 3:
                low_rows[k, x, :, 0:128] = a
                low_rows[k, x, :, 128:256] = b
            if x > 12:
                high_rows[k, x - 13, :, 0:128] = a
                high_rows[k, x - 13, :, 128:256] = b
            turned_a = pltpu.roll(a, 8 * x, 1) if x else a
            turned_b = pltpu.roll(b, (8 * x + 8) % 128, 1) if x < 15 else b
            left = jnp.where(slot == x, turned_a, left)
            right = jnp.where(slot == x, turned_b, right)
        low_columns[k] = left
        high_columns[k] = right
        return carry

    lax.fori_loop(0, 9, each, 0)


def edges(u):
    rows = jax.ShapeDtypeStruct((9, 3, 16, 256), f32)
    columns = jax.ShapeDtypeStruct((9, 16, 128), f32)
    return pl.pallas_call(edges_body, out_shape=(rows, rows, columns, columns), name="edges")(u)


def tendency(below, row, above, reach, spacing):
    width = row[0].shape[-1]
    square = 1.0 / (spacing * spacing)
    out = []
    for c in range(3):
        u = row[c]
        up = pltpu.roll(u, 15, 0)
        down = pltpu.roll(u, 1, 0)
        north = pltpu.roll(u, width - reach, 1)
        south = pltpu.roll(u, reach, 1)
        laplace = (above[c] + below[c]) + (up + down) - (4.0 + 2.0 * square) * u
        laplace = laplace + (north + south) * square
        transport = (
            row[0] * (above[c] - below[c])
            + row[1] * ((north - south) * (1.0 / spacing))
            + row[2] * (up - down)
        )
        out.append(viscosity * laplace - 0.5 * transport)
    return out


def fine_body(place, u, before, after, south_0, south_1, south_2, north_0, north_1, north_2,
              sources, halves_1, halves_2, ue, v1, v2, rest, f0, h1, pair_u, pair_v, native_0, native_1):
    gx = place[0]
    gy = place[1]
    leader = place[2] == 0
    lane = lanes((16, 128))
    wide = lanes((16, 384))
    even = wide % 2 == 0
    low_ok = jnp.where(gx > 0, 1.0, 0.0).astype(f32)
    high_ok = jnp.where(gx < 3, 1.0, 0.0).astype(f32)
    north_ok = jnp.where(gy < 3, 1.0, 0.0).astype(f32)
    south_ok = jnp.where(gy > 0, 1.0, 0.0).astype(f32)
    columns_ok = jnp.where(wide < 256, 1.0, jnp.where(wide < 320, north_ok, south_ok))

    def gather(k, carry):
        for e in range(22):
            x = e - 3
            if x < 0:
                ue[k, e, :, 0:256] = before[k, e]
                a, b, slot = north_0, south_0, 16 + x
            elif x < 16:
                ue[k, e, :, 0:128] = strided(u, k, x, 0)
                ue[k, e, :, 128:256] = strided(u, k, x, 1)
                a, b, slot = north_1, south_1, x
            else:
                ue[k, e, :, 0:256] = after[k, x - 16]
                a, b, slot = north_2, south_2, x - 16
            a = a[k]
            b = b[k]
            if slot > 0:
                a = pltpu.roll(a, 128 - 8 * slot, 1)
            if slot < 15:
                b = pltpu.roll(b, 120 - 8 * slot, 1)
            ue[k, e, :, 256:384] = jnp.where(lane < 64, a, b)
        return carry

    lax.fori_loop(0, 9, gather, 0)

    def row_ok(e):
        return jnp.where(e < 3, low_ok, jnp.where(e > 18, high_ok, 1.0))

    def paired(field):
        return 0.5 * (field + jnp.where(even, pltpu.roll(field, 383, 1), pltpu.roll(field, 1, 1)))

    def first(e, carry):
        flux = []
        for node in range(3):
            rows = [[ue[3 * node + c, e + d] for c in range(3)] for d in (-1, 0, 1)]
            flux.append(tendency(*rows, 1, 1.0))
        ok = columns_ok * row_ok(e)
        for c in range(3):
            a, b, d = flux[0][c], flux[1][c], flux[2][c]
            start = ue[c, e]
            new = start + slice_step * (first_row[0] * a + first_row[1] * b + first_row[2] * d)
            new = new * ok
            v1[c, e] = new
            rest[c, e] = (
                slice_step * (second_row[0] * a + second_row[1] * b + second_row[2] * d)
                - half_step * b
            )
            f0[c, e] = a
            pair_u[c, e] = paired(start)
            pair_v[c, e] = paired(new)
        return carry

    lax.fori_loop(1, 21, first, 0)

    def second(e, carry):
        rows = [[v1[c, e + d] for c in range(3)] for d in (-1, 0, 1)]
        slope = tendency(*rows, 1, 1.0)
        ok = columns_ok * row_ok(e)
        for c in range(3):
            v2[c, e] = (rows[1][c] + half_step * slope[c] + rest[c, e]) * ok
            h1[c, e] = slope[c]
        return carry

    lax.fori_loop(2, 20, second, 0)

    def put(field, c, x, value):
        at = pl.ds((field * 3 + c) * 256 + x, 16, stride=16)
        native_0[at, :] = value[:, 0:128]
        native_1[at, :] = value[:, 128:256]

    def third(e, carry):
        rows = [[v2[c, e + d] for c in range(3)] for d in (-1, 0, 1)]
        slope = tendency(*rows, 1, 1.0)
        base_u = tendency(*[[pair_u[c, e + d] for c in range(3)] for d in (-1, 0, 1)], 2, 2.0)
        base_v = tendency(*[[pair_v[c, e + d] for c in range(3)] for d in (-1, 0, 1)], 2, 2.0)
        for c in range(3):
            a, b, d = f0[c, e], h1[c, e], slope[c]
            one = slice_step * (first_row[0] * a + first_row[1] * b + first_row[2] * d)
            two = slice_step * (second_row[0] * a + second_row[1] * b + second_row[2] * d)
            one = one + jnp.where(leader, ue[c, e], -half_step * base_u[c])
            two = two - half_step * base_v[c]
            put(0, c, e - 3, one)
            put(1, c, e - 3, two)
            put(2, c, e - 3, v1[c, e])
            put(3, c, e - 3, rows[1][c])
        return carry

    lax.fori_loop(3, 19, third, 0)

    fine = lanes((64, 128))
    own = fine // 2 == lax.broadcasted_iota(jnp.int32, (64, 128), 0)
    mean = jnp.where(own, 0.5, 0.0).astype(f32)
    half = jnp.where(own, jnp.where(fine % 2 == 0, 0.5, -0.5), 0.0).astype(f32)

    def contract(matrix, part, out, at):
        for native, to in ((native_0, 0), (native_1, 64)):
            out[to:to + 64, at:at + 256] = lax.dot_general(
                matrix, native[part * 256:(part + 1) * 256, :], (((1,), (1,)), ((), ())),
                precision=highest, preferred_element_type=f32,
            )

    for part in range(6):
        contract(mean, part, sources, part * 256)
    for part in range(3):
        contract(half, 6 + part, halves_1, part * 256)
        contract(half, 9 + part, halves_2, part * 256)


def fine_part(place, *arrays):
    vmem = pl.BlockSpec(memory_space=pltpu.VMEM)
    field = pltpu.VMEM((3, 22, 16, 384), f32)
    return pl.pallas_call(
        fine_body,
        out_shape=(
            jax.ShapeDtypeStruct((128, 1536), f32),
            jax.ShapeDtypeStruct((128, 768), f32),
            jax.ShapeDtypeStruct((128, 768), f32),
        ),
        in_specs=[pl.BlockSpec(memory_space=pltpu.SMEM)] + [vmem] * len(arrays),
        scratch_shapes=[pltpu.VMEM((9, 22, 16, 384), f32)] + [field] * 7 + [pltpu.VMEM((3072, 128), f32)] * 2,
        compiler_params=pltpu.CompilerParams(vmem_limit_bytes=60 * 2**20),
        name="fine",
    )(place, *arrays)


def stage_body(place, own, left, right, source, source_left, source_right, *rest):
    *outs, buffer_0, buffer_1 = rest
    last = outs[0]
    trace = outs[1] if len(outs) > 1 else None
    lane = lanes((24, 128))
    x_first = lane % 16 == 0
    x_last = lane % 16 == 15
    z_first = lane < 16
    z_last = lane >= 112
    row = lax.broadcasted_iota(jnp.int32, (24, 128), 0)
    inside = ((row >= 8) | (place[3] > 0)) & ((row < 16) | (place[3] < 63))

    for c in range(3):
        for t in range(8):
            buffer_0[c, t, 0:8] = left[c, t]
            buffer_0[c, t, 8:16] = own[c, t]
            buffer_0[c, t, 16:24] = right[c, t]

    def keep(j, field, buffer):
        for xh in range(4):
            for c in range(3):
                for zh in range(2):
                    at = (field * 6 + c * 2 + zh) * 128
                    trace[j * 4 + xh, :, at:at + 128] = buffer[c, xh * 2 + zh, 8:16]

    square = 0.25
    c_side = half_step * viscosity
    c_second = half_step * viscosity * square
    c_centre = 1.0 - half_step * viscosity * (4.0 + 2.0 * square)

    def step(j, field, old, new):
        for xh in range(4):
            u = [[old[c, 2 * xh + zh] for zh in range(2)] for c in range(3)]
            for zh in range(2):
                t = 2 * xh + zh
                k0 = u[0][zh] * (-0.5 * half_step)
                k1 = u[1][zh] * (-0.25 * half_step)
                k2 = u[2][zh] * (-0.5 * half_step)
                for c in range(3):
                    v = u[c][zh]
                    o = u[c][1 - zh]
                    after = pltpu.roll(old[c, t + 2], 15, 1) if xh < 3 else jnp.zeros((24, 128), f32)
                    before = pltpu.roll(old[c, t - 2], 113, 1) if xh > 0 else jnp.zeros((24, 128), f32)
                    east = jnp.where(x_last, after, pltpu.roll(v, 127, 1))
                    west = jnp.where(x_first, before, pltpu.roll(v, 1, 1))
                    up = jnp.where(z_last, pltpu.roll(o, 112, 1), pltpu.roll(v, 112, 1))
                    down = jnp.where(z_first, pltpu.roll(o, 16, 1), pltpu.roll(v, 16, 1))
                    north = pltpu.roll(v, 23, 0)
                    south = pltpu.roll(v, 1, 0)
                    at = (field * 6 + c * 2 + zh) * 128
                    pull = jnp.concatenate(
                        [r[j * 4 + xh, :, at:at + 128] for r in (source_left, source, source_right)], axis=0
                    )
                    value = (
                        c_centre * v
                        + c_side * ((east + west) + (up + down))
                        + c_second * (north + south)
                        + (k0 * (east - west) + k1 * (north - south) + k2 * (up - down))
                        + pull
                    )
                    new[c, t] = jnp.where(inside, value, 0.0)

    def one_slice(j, carry):
        if trace is not None:
            keep(j, 0, buffer_0)
        step(j, 0, buffer_0, buffer_1)
        if trace is not None:
            keep(j, 1, buffer_1)
        step(j, 1, buffer_1, buffer_0)
        if trace is not None:
            keep(j, 2, buffer_0)
        return carry

    lax.fori_loop(0, 4, one_slice, 0)
    for c in range(3):
        for t in range(8):
            last[c, t] = buffer_0[c, t, 8:16]


def stage(place, own, left, right, source, source_left, source_right, keeps):
    vmem = pl.BlockSpec(memory_space=pltpu.VMEM)
    shapes = [jax.ShapeDtypeStruct((3, 8, 8, 128), f32)]
    if keeps:
        shapes.append(jax.ShapeDtypeStruct((16, 8, 2304), f32))
    return pl.pallas_call(
        stage_body,
        out_shape=shapes,
        in_specs=[pl.BlockSpec(memory_space=pltpu.SMEM)] + [vmem] * 6,
        scratch_shapes=[pltpu.VMEM((3, 8, 24, 128), f32)] * 2,
        compiler_params=pltpu.CompilerParams(vmem_limit_bytes=60 * 2**20),
        name="stage",
    )(place, own, left, right, source, source_left, source_right)


def finish_body(place, start, coarse, halves_0, halves_1, halves_2, out):
    fine = lanes((128, 128))
    k = lax.broadcasted_iota(jnp.int32, (128, 128), 0)
    sign = jnp.where(k < 64, 1.0, jnp.where(fine % 2 == 0, 1.0, -1.0))
    matrix = jnp.where(fine // 2 == k % 64, sign, 0.0).astype(f32)
    for field, halves in enumerate((halves_0, halves_1, halves_2)):
        for c in range(3):
            at = field * 768 + c * 256
            for half in range(2):
                part = pl.ds(half * 64, 64)
                both = jnp.concatenate(
                    [coarse[part, at:at + 256], halves[part, c * 256:(c + 1) * 256]], axis=0
                )
                value = lax.dot_general(
                    both.T, matrix, (((1,), (0,)), ((), ())), precision=highest, preferred_element_type=f32
                )
                out[at // 8:at // 8 + 32, half] = value.reshape(32, 8, 128)

    @pl.when(place[2] == 0)
    def _():
        pltpu.sync_copy(start.at[pl.ds(0, 96)], out.at[pl.ds(0, 96)])


def finish(place, start, coarse, halves_0, halves_1, halves_2):
    vmem = pl.BlockSpec(memory_space=pltpu.VMEM)
    return pl.pallas_call(
        finish_body,
        out_shape=jax.ShapeDtypeStruct((288, 2, 8, 128), f32),
        in_specs=[pl.BlockSpec(memory_space=pltpu.SMEM), pl.BlockSpec(memory_space=pl.ANY)] + [vmem] * 4,
        compiler_params=pltpu.CompilerParams(vmem_limit_bytes=60 * 2**20),
        name="finish",
    )(place, start, coarse, halves_0, halves_1, halves_2)


def sent(block, axes, sizes, moves):
    strides = {}
    total = 1
    for axis in reversed(axes):
        strides[axis] = total
        total *= sizes[axis]
    pairs = []
    for source in range(total):
        target = source
        for axis, by in moves.items():
            at = source // strides[axis] % sizes[axis]
            if not 0 <= at + by < sizes[axis]:
                target = None
                break
            target += by * strides[axis]
        if target is not None:
            pairs.append((source, target))
    return lax.ppermute(block, axes if len(axes) > 1 else axes[0], pairs)


def solution(mesh):
    sizes = {"tz": 4, "ty": 4, "gx": 4, "gy": 4}
    fine_mesh = Mesh(mesh.devices.reshape(4, 4, 4, 4), tuple(sizes))
    lateral = ("gx", "gy")
    pieces = ("ty", "gx", "gy")

    def beside(block, by):
        name = lambda piece: (piece % 16) * 4 + piece // 16
        pairs = [(name(i), name(i + by)) for i in range(64) if 0 <= i + by < 64]
        return lax.ppermute(block, pieces, pairs)

    def per_device(provisional):
        tz, ty, gx, gy = (lax.axis_index(a) for a in sizes)
        place = jnp.stack([gx, gy, tz * 4 + ty, gy * 16 + ty * 4 + gx]).astype(jnp.int32)
        tiles = provisional.reshape(288, 8, 2, 128).transpose(0, 2, 1, 3)
        u = tiles.reshape(4608, 128)
        low_rows, high_rows, low_columns, high_columns = edges(u)
        after = sent(low_rows, lateral, sizes, {"gx": -1})
        before = sent(high_rows, lateral, sizes, {"gx": 1})
        south = [sent(high_columns, lateral, sizes, {"gx": -d, "gy": 1}) for d in (-1, 0, 1)]
        north = [sent(low_columns, lateral, sizes, {"gx": -d, "gy": -1}) for d in (-1, 0, 1)]
        sources, halves_1, halves_2 = fine_part(place, u, before, after, *south, *north)
        halves_0 = lax.ppermute(halves_2, ("tz", "ty"), [(i, i + 1) for i in range(15)])
        source = lax.all_to_all(sources.reshape(16, 8, 1536), group_axes, 0, 0)
        source_left = beside(source, 1)
        source_right = beside(source, -1)
        own = left = right = jnp.zeros((3, 8, 8, 128), f32)
        for turn in range(4):
            own, *kept = stage(place, own, left, right, source, source_left, source_right, turn == 3)
            if turn < 3:
                own = sent(own, ("tz",), sizes, {"tz": 1})
                left = beside(own, 1)
                right = beside(own, -1)
        coarse = lax.all_to_all(kept[0], group_axes, 0, 0).reshape(128, 2304)
        out = finish(place, tiles, coarse, halves_0, halves_1, halves_2)
        return out.transpose(0, 2, 1, 3).reshape(1, 3, 3, 16, 16, 256)

    spec = P(("tz", "ty"), None, None, None, "gx", "gy")
    return jax.shard_map(per_device, mesh=fine_mesh, in_specs=(spec,), out_specs=spec, check_vma=False)
```

```python
import jax
import jax.numpy as jnp
from jax import lax
from jax.experimental import pallas as pl
from jax.experimental.pallas import tpu as pltpu
from jax.sharding import Mesh
from jax.sharding import PartitionSpec as P


viscosity = 0.1
slice_step = 0.25
half_step = 0.125
first_row = (5.0 / 24.0, 1.0 / 3.0, -1.0 / 24.0)
second_row = (-1.0 / 24.0, 1.0 / 3.0, 5.0 / 24.0)

f32 = jnp.float32
highest = lax.Precision.HIGHEST
group_axes = ("ty", "gx")


def lanes(shape):
    return lax.broadcasted_iota(jnp.int32, shape, len(shape) - 1)


def strided(u, k, x, half):
    return u[pl.ds(k * 512 + x // 8 * 16 + half * 8 + x % 8, 16, stride=32), :]


def edges_body(u, low_rows, high_rows, low_columns, high_columns):
    slot = lanes((16, 128)) // 8

    def each(k, carry):
        left = jnp.zeros((16, 128), f32)
        right = jnp.zeros((16, 128), f32)
        for x in range(16):
            a = strided(u, k, x, 0)
            b = strided(u, k, x, 1)
            if x < 3:
                low_rows[k, x, :, 0:128] = a
                low_rows[k, x, :, 128:256] = b
            if x > 12:
                high_rows[k, x - 13, :, 0:128] = a
                high_rows[k, x - 13, :, 128:256] = b
            turned_a = pltpu.roll(a, 8 * x, 1) if x else a
            turned_b = pltpu.roll(b, (8 * x + 8) % 128, 1) if x < 15 else b
            left = jnp.where(slot == x, turned_a, left)
            right = jnp.where(slot == x, turned_b, right)
        low_columns[k] = left
        high_columns[k] = right
        return carry

    lax.fori_loop(0, 9, each, 0)


def edges(u):
    rows = jax.ShapeDtypeStruct((9, 3, 16, 256), f32)
    columns = jax.ShapeDtypeStruct((9, 16, 128), f32)
    return pl.pallas_call(edges_body, out_shape=(rows, rows, columns, columns), name="edges")(u)


def corners_body(south, north, up, down):
    lane = lanes((16, 128))
    for k in range(9):
        turned = pltpu.roll(north[k], 64, 1)
        up[k] = jnp.where(lane >= 64, south[k], turned)
        down[k] = jnp.where(lane < 64, south[k], turned)


def corners(south, north):
    shape = jax.ShapeDtypeStruct((9, 16, 128), f32)
    return pl.pallas_call(corners_body, out_shape=(shape, shape), name="corners")(south, north)


def tendency(below, row, above, reach, spacing):
    width = row[0].shape[-1]
    square = 1.0 / (spacing * spacing)
    out = []
    for c in range(3):
        u = row[c]
        up = pltpu.roll(u, 15, 0)
        down = pltpu.roll(u, 1, 0)
        north = pltpu.roll(u, width - reach, 1)
        south = pltpu.roll(u, reach, 1)
        laplace = (above[c] + below[c]) + (up + down) - (4.0 + 2.0 * square) * u
        laplace = laplace + (north + south) * square
        transport = (
            row[0] * (above[c] - below[c])
            + row[1] * ((north - south) * (1.0 / spacing))
            + row[2] * (up - down)
        )
        out.append(viscosity * laplace - 0.5 * transport)
    return out


def fine_body(place, u, before, after, south, north, corner_before, corner_after,
              sources, halves_1, halves_2, ue, v1, v2, rest, f0, h1, pair_u, pair_v, native_0, native_1):
    gx = place[0]
    gy = place[1]
    leader = place[2] == 0
    lane = lanes((16, 128))
    wide = lanes((16, 384))
    even = wide % 2 == 0
    low_ok = jnp.where(gx > 0, 1.0, 0.0).astype(f32)
    high_ok = jnp.where(gx < 3, 1.0, 0.0).astype(f32)
    north_ok = jnp.where(gy < 3, 1.0, 0.0).astype(f32)
    south_ok = jnp.where(gy > 0, 1.0, 0.0).astype(f32)
    columns_ok = jnp.where(wide < 256, 1.0, jnp.where(wide < 320, north_ok, south_ok))

    def gather(k, carry):
        for e in range(22):
            x = e - 3
            if x < 0:
                ue[k, e, :, 0:256] = before[k, e]
                a, b, slot_a, slot_b = corner_before, corner_before, 8 + x, 16 + x
            elif x < 16:
                ue[k, e, :, 0:128] = strided(u, k, x, 0)
                ue[k, e, :, 128:256] = strided(u, k, x, 1)
                a, b, slot_a, slot_b = north, south, x, x
            else:
                ue[k, e, :, 0:256] = after[k, x - 16]
                a, b, slot_a, slot_b = corner_after, corner_after, x - 8, x - 16
            a = a[k]
            b = b[k]
            if slot_a > 0:
                a = pltpu.roll(a, 128 - 8 * slot_a, 1)
            if slot_b < 15:
                b = pltpu.roll(b, 120 - 8 * slot_b, 1)
            ue[k, e, :, 256:384] = jnp.where(lane < 64, a, b)
        return carry

    lax.fori_loop(0, 9, gather, 0)

    def row_ok(e):
        return jnp.where(e < 3, low_ok, jnp.where(e > 18, high_ok, 1.0))

    def paired(field):
        return 0.5 * (field + jnp.where(even, pltpu.roll(field, 383, 1), pltpu.roll(field, 1, 1)))

    def first(e, carry):
        flux = []
        for node in range(3):
            rows = [[ue[3 * node + c, e + d] for c in range(3)] for d in (-1, 0, 1)]
            flux.append(tendency(*rows, 1, 1.0))
        ok = columns_ok * row_ok(e)
        for c in range(3):
            a, b, d = flux[0][c], flux[1][c], flux[2][c]
            start = ue[c, e]
            new = start + slice_step * (first_row[0] * a + first_row[1] * b + first_row[2] * d)
            new = new * ok
            v1[c, e] = new
            rest[c, e] = (
                slice_step * (second_row[0] * a + second_row[1] * b + second_row[2] * d)
                - half_step * b
            )
            f0[c, e] = a
            pair_u[c, e] = paired(start)
            pair_v[c, e] = paired(new)
        return carry

    lax.fori_loop(1, 21, first, 0)

    def second(e, carry):
        rows = [[v1[c, e + d] for c in range(3)] for d in (-1, 0, 1)]
        slope = tendency(*rows, 1, 1.0)
        ok = columns_ok * row_ok(e)
        for c in range(3):
            v2[c, e] = (rows[1][c] + half_step * slope[c] + rest[c, e]) * ok
            h1[c, e] = slope[c]
        return carry

    lax.fori_loop(2, 20, second, 0)

    def put(field, c, x, value):
        at = pl.ds((field * 3 + c) * 256 + x, 16, stride=16)
        native_0[at, :] = value[:, 0:128]
        native_1[at, :] = value[:, 128:256]

    def third(e, carry):
        rows = [[v2[c, e + d] for c in range(3)] for d in (-1, 0, 1)]
        slope = tendency(*rows, 1, 1.0)
        base_u = tendency(*[[pair_u[c, e + d] for c in range(3)] for d in (-1, 0, 1)], 2, 2.0)
        base_v = tendency(*[[pair_v[c, e + d] for c in range(3)] for d in (-1, 0, 1)], 2, 2.0)
        for c in range(3):
            a, b, d = f0[c, e], h1[c, e], slope[c]
            one = slice_step * (first_row[0] * a + first_row[1] * b + first_row[2] * d)
            two = slice_step * (second_row[0] * a + second_row[1] * b + second_row[2] * d)
            one = one + jnp.where(leader, ue[c, e], -half_step * base_u[c])
            two = two - half_step * base_v[c]
            put(0, c, e - 3, one)
            put(1, c, e - 3, two)
            put(2, c, e - 3, v1[c, e])
            put(3, c, e - 3, rows[1][c])
        return carry

    lax.fori_loop(3, 19, third, 0)

    fine = lanes((64, 128))
    own = fine // 2 == lax.broadcasted_iota(jnp.int32, (64, 128), 0)
    mean = jnp.where(own, 0.5, 0.0).astype(f32)
    half = jnp.where(own, jnp.where(fine % 2 == 0, 0.5, -0.5), 0.0).astype(f32)

    def contract(matrix, part, out, at):
        for native, to in ((native_0, 0), (native_1, 64)):
            out[to:to + 64, at:at + 256] = lax.dot_general(
                matrix, native[part * 256:(part + 1) * 256, :], (((1,), (1,)), ((), ())),
                precision=highest, preferred_element_type=f32,
            )

    for part in range(6):
        contract(mean, part, sources, part * 256)
    for part in range(3):
        contract(half, 6 + part, halves_1, part * 256)
        contract(half, 9 + part, halves_2, part * 256)


def fine_part(place, *arrays):
    vmem = pl.BlockSpec(memory_space=pltpu.VMEM)
    field = pltpu.VMEM((3, 22, 16, 384), f32)
    return pl.pallas_call(
        fine_body,
        out_shape=(
            jax.ShapeDtypeStruct((128, 1536), f32),
            jax.ShapeDtypeStruct((128, 768), f32),
            jax.ShapeDtypeStruct((128, 768), f32),
        ),
        in_specs=[pl.BlockSpec(memory_space=pltpu.SMEM)] + [vmem] * len(arrays),
        scratch_shapes=[pltpu.VMEM((9, 22, 16, 384), f32)] + [field] * 7 + [pltpu.VMEM((3072, 128), f32)] * 2,
        compiler_params=pltpu.CompilerParams(vmem_limit_bytes=60 * 2**20),
        name="fine",
    )(place, *arrays)


def pack_body(source, to_right, to_left):
    row = lax.broadcasted_iota(jnp.int32, (8, 768), 0)
    for j in range(2):
        for field in range(2):
            k = 2 * j + field
            for xh in range(4):
                one = source[j * 4 + xh, :, field * 768:(field + 1) * 768]
                two = source[(3 - j) * 4 + xh, :, (1 - field) * 768:(2 - field) * 768]
                right = pltpu.roll(two, k, 0) if k else two
                left = pltpu.roll(two, 8 - k, 0) if k else two
                to_right[j * 4 + xh, :, field * 768:(field + 1) * 768] = jnp.where(row > k, one, right)
                to_left[j * 4 + xh, :, field * 768:(field + 1) * 768] = jnp.where(row < 7 - k, one, left)


def pack(source):
    shape = jax.ShapeDtypeStruct((8, 8, 1536), f32)
    return pl.pallas_call(pack_body, out_shape=(shape, shape), name="pack")(source)


def stage_body(place, own, left, right, source, source_left, source_right, *rest):
    *outs, buffer_0, buffer_1 = rest
    last = outs[0]
    trace = outs[1] if len(outs) > 1 else None
    lane = lanes((24, 128))
    x_first = lane % 16 == 0
    x_last = lane % 16 == 15
    z_first = lane < 16
    z_last = lane >= 112
    row = lax.broadcasted_iota(jnp.int32, (24, 128), 0)
    inside = ((row >= 8) | (place[3] > 0)) & ((row < 16) | (place[3] < 63))

    for c in range(3):
        for t in range(8):
            buffer_0[c, t, 0:8] = left[c, t]
            buffer_0[c, t, 8:16] = own[c, t]
            buffer_0[c, t, 16:24] = right[c, t]

    def keep(j, field, buffer):
        for xh in range(4):
            for c in range(3):
                for zh in range(2):
                    at = (field * 6 + c * 2 + zh) * 128
                    trace[j * 4 + xh, :, at:at + 128] = buffer[c, xh * 2 + zh, 8:16]

    square = 0.25
    c_side = half_step * viscosity
    c_second = half_step * viscosity * square
    c_centre = 1.0 - half_step * viscosity * (4.0 + 2.0 * square)

    def step(j, field, old, new, late):
        k = 2 * j + field
        for xh in range(4):
            u = [[old[c, 2 * xh + zh] for zh in range(2)] for c in range(3)]
            for zh in range(2):
                t = 2 * xh + zh
                k0 = u[0][zh] * (-0.5 * half_step)
                k1 = u[1][zh] * (-0.25 * half_step)
                k2 = u[2][zh] * (-0.5 * half_step)
                for c in range(3):
                    v = u[c][zh]
                    o = u[c][1 - zh]
                    after = pltpu.roll(old[c, t + 2], 15, 1) if xh < 3 else jnp.zeros((24, 128), f32)
                    before = pltpu.roll(old[c, t - 2], 113, 1) if xh > 0 else jnp.zeros((24, 128), f32)
                    east = jnp.where(x_last, after, pltpu.roll(v, 127, 1))
                    west = jnp.where(x_first, before, pltpu.roll(v, 1, 1))
                    up = jnp.where(z_last, pltpu.roll(o, 112, 1), pltpu.roll(v, 112, 1))
                    down = jnp.where(z_first, pltpu.roll(o, 16, 1), pltpu.roll(v, 16, 1))
                    north = pltpu.roll(v, 23, 0)
                    south = pltpu.roll(v, 1, 0)
                    at = (field * 6 + c * 2 + zh) * 128
                    if late:
                        there = ((1 - field) * 6 + c * 2 + zh) * 128
                        pull_left = pltpu.roll(source_left[(3 - j) * 4 + xh, :, there:there + 128], 1 + k, 0)
                        pull_right = pltpu.roll(source_right[(3 - j) * 4 + xh, :, there:there + 128], 7 - k, 0)
                    else:
                        pull_left = source_left[j * 4 + xh, :, at:at + 128]
                        pull_right = source_right[j * 4 + xh, :, at:at + 128]
                    pull = jnp.concatenate(
                        [pull_left, source[j * 4 + xh, :, at:at + 128], pull_right], axis=0
                    )
                    value = (
                        c_centre * v
                        + c_side * ((east + west) + (up + down))
                        + c_second * (north + south)
                        + (k0 * (east - west) + k1 * (north - south) + k2 * (up - down))
                        + pull
                    )
                    new[c, t] = jnp.where(inside, value, 0.0)

    def one_slice(j, late):
        if trace is not None:
            keep(j, 0, buffer_0)
        step(j, 0, buffer_0, buffer_1, late)
        if trace is not None:
            keep(j, 1, buffer_1)
        step(j, 1, buffer_1, buffer_0, late)
        if trace is not None:
            keep(j, 2, buffer_0)
        return late

    lax.fori_loop(0, 2, lambda j, carry: one_slice(j, False) or carry, 0)
    lax.fori_loop(2, 4, lambda j, carry: (one_slice(j, True), carry)[1], 0)
    for c in range(3):
        for t in range(8):
            last[c, t] = buffer_0[c, t, 8:16]


def stage(place, own, left, right, source, source_left, source_right, keeps):
    vmem = pl.BlockSpec(memory_space=pltpu.VMEM)
    shapes = [jax.ShapeDtypeStruct((3, 8, 8, 128), f32)]
    if keeps:
        shapes.append(jax.ShapeDtypeStruct((16, 8, 2304), f32))
    return pl.pallas_call(
        stage_body,
        out_shape=shapes,
        in_specs=[pl.BlockSpec(memory_space=pltpu.SMEM)] + [vmem] * 6,
        scratch_shapes=[pltpu.VMEM((3, 8, 24, 128), f32)] * 2,
        compiler_params=pltpu.CompilerParams(vmem_limit_bytes=60 * 2**20),
        name="stage",
    )(place, own, left, right, source, source_left, source_right)


def finish_body(place, start, coarse, halves_0, halves_1, halves_2, out):
    fine = lanes((128, 128))
    k = lax.broadcasted_iota(jnp.int32, (128, 128), 0)
    sign = jnp.where(k < 64, 1.0, jnp.where(fine % 2 == 0, 1.0, -1.0))
    matrix = jnp.where(fine // 2 == k % 64, sign, 0.0).astype(f32)
    for field, halves in enumerate((halves_0, halves_1, halves_2)):
        for c in range(3):
            at = field * 768 + c * 256
            for half in range(2):
                part = pl.ds(half * 64, 64)
                both = jnp.concatenate(
                    [coarse[part, at:at + 256], halves[part, c * 256:(c + 1) * 256]], axis=0
                )
                value = lax.dot_general(
                    both.T, matrix, (((1,), (0,)), ((), ())), precision=highest, preferred_element_type=f32
                )
                out[at // 8:at // 8 + 32, half] = value.reshape(32, 8, 128)

    @pl.when(place[2] == 0)
    def _():
        pltpu.sync_copy(start.at[pl.ds(0, 96)], out.at[pl.ds(0, 96)])


def finish(place, start, coarse, halves_0, halves_1, halves_2):
    vmem = pl.BlockSpec(memory_space=pltpu.VMEM)
    return pl.pallas_call(
        finish_body,
        out_shape=jax.ShapeDtypeStruct((288, 2, 8, 128), f32),
        in_specs=[pl.BlockSpec(memory_space=pltpu.SMEM), pl.BlockSpec(memory_space=pl.ANY)] + [vmem] * 4,
        compiler_params=pltpu.CompilerParams(vmem_limit_bytes=60 * 2**20),
        name="finish",
    )(place, start, coarse, halves_0, halves_1, halves_2)


def sent(block, axes, sizes, moves):
    strides = {}
    total = 1
    for axis in reversed(axes):
        strides[axis] = total
        total *= sizes[axis]
    pairs = []
    for source in range(total):
        target = source
        for axis, by in moves.items():
            at = source // strides[axis] % sizes[axis]
            if not 0 <= at + by < sizes[axis]:
                target = None
                break
            target += by * strides[axis]
        if target is not None:
            pairs.append((source, target))
    return lax.ppermute(block, axes if len(axes) > 1 else axes[0], pairs)


def solution(mesh):
    sizes = {"tz": 4, "ty": 4, "gx": 4, "gy": 4}
    fine_mesh = Mesh(mesh.devices.reshape(4, 4, 4, 4), tuple(sizes))
    pieces = ("ty", "gx", "gy")

    def beside(block, by):
        name = lambda piece: (piece % 16) * 4 + piece // 16
        pairs = [(name(i), name(i + by)) for i in range(64) if 0 <= i + by < 64]
        return lax.ppermute(block, pieces, pairs)

    def per_device(provisional):
        tz, ty, gx, gy = (lax.axis_index(a) for a in sizes)
        place = jnp.stack([gx, gy, tz * 4 + ty, gy * 16 + ty * 4 + gx]).astype(jnp.int32)
        tiles = provisional.reshape(288, 8, 2, 128).transpose(0, 2, 1, 3)
        u = tiles.reshape(4608, 128)
        low_rows, high_rows, low_columns, high_columns = edges(u)
        after = sent(low_rows, ("gx",), sizes, {"gx": -1})
        before = sent(high_rows, ("gx",), sizes, {"gx": 1})
        south = sent(high_columns, ("gy",), sizes, {"gy": 1})
        north = sent(low_columns, ("gy",), sizes, {"gy": -1})
        up, down = corners(south, north)
        corner_before = sent(up, ("gx",), sizes, {"gx": 1})
        corner_after = sent(down, ("gx",), sizes, {"gx": -1})
        sources, halves_1, halves_2 = fine_part(
            place, u, before, after, south, north, corner_before, corner_after
        )
        halves_0 = lax.ppermute(halves_2, ("tz", "ty"), [(i, i + 1) for i in range(15)])
        source = lax.all_to_all(sources.reshape(16, 8, 1536), group_axes, 0, 0)
        to_right, to_left = pack(source)
        source_left = beside(to_right, 1)
        source_right = beside(to_left, -1)
        own = left = right = jnp.zeros((3, 8, 8, 128), f32)
        for turn in range(4):
            own, *kept = stage(place, own, left, right, source, source_left, source_right, turn == 3)
            if turn < 3:
                own = sent(own, ("tz",), sizes, {"tz": 1})
                left = beside(own, 1)
                right = beside(own, -1)
        coarse = lax.all_to_all(kept[0], group_axes, 0, 0).reshape(128, 2304)
        out = finish(place, tiles, coarse, halves_0, halves_1, halves_2)
        return out.transpose(0, 2, 1, 3).reshape(1, 3, 3, 16, 16, 256)

    spec = P(("tz", "ty"), None, None, None, "gx", "gy")

    return jax.shard_map(per_device, mesh=fine_mesh, in_specs=(spec,), out_specs=spec, check_vma=False)
```

```python
import functools

import jax
import jax.numpy as jnp
from jax import lax
from jax.experimental import pallas as pl
from jax.experimental.pallas import tpu as pltpu
from jax.sharding import Mesh
from jax.sharding import PartitionSpec as P


viscosity = 0.1
slice_step = 0.25
half_step = 0.125
first_row = (5.0 / 24.0, 1.0 / 3.0, -1.0 / 24.0)
second_row = (-1.0 / 24.0, 1.0 / 3.0, 5.0 / 24.0)

f32 = jnp.float32
group_axes = ("ty", "gx")


def near(*arrays):
    return tuple(pltpu.with_memory_space_constraint(a, pltpu.VMEM) for a in arrays)


def lanes(shape):
    return lax.broadcasted_iota(jnp.int32, shape, len(shape) - 1)


def strided(u, k, x, half):
    at = k * 512 + x // 8 * 16 + half * 8 + x % 8
    return jnp.concatenate([u[pl.ds(at + 32 * odd, 8, stride=64), :] for odd in (0, 1)], axis=0)


def edges_body(u, low_rows, high_rows, low_columns, high_columns):
    slot = lanes((16, 128)) // 8
    k = pl.program_id(0)
    left = jnp.zeros((16, 128), f32)
    right = jnp.zeros((16, 128), f32)
    for x in range(16):
        a = strided(u, 0, x, 0)
        b = strided(u, 0, x, 1)
        if x < 3:
            low_rows[k, x, :, 0:128] = a
            low_rows[k, x, :, 128:256] = b
        if x > 12:
            high_rows[k, x - 13, :, 0:128] = a
            high_rows[k, x - 13, :, 128:256] = b
        turned_a = pltpu.roll(a, 8 * x, 1) if x else a
        turned_b = pltpu.roll(b, (8 * x + 8) % 128, 1) if x < 15 else b
        left = jnp.where(slot == x, turned_a, left)
        right = jnp.where(slot == x, turned_b, right)
    low_columns[k] = left
    high_columns[k] = right


def edges(u):
    vmem = pl.BlockSpec(memory_space=pltpu.VMEM)
    rows = pltpu.VMEM((9, 3, 16, 256), f32)
    columns = pltpu.VMEM((9, 16, 128), f32)
    return pl.pallas_call(
        edges_body,
        grid=(9,),
        in_specs=[pl.BlockSpec((512, 128), lambda k: (k, 0))],
        out_specs=[vmem] * 4,
        out_shape=(rows, rows, columns, columns),
        compiler_params=pltpu.CompilerParams(vmem_limit_bytes=8 * 2**20),
        name="edges",
    )(u)


def corners_body(south, north, up, down):
    lane = lanes((16, 128))
    for k in range(9):
        turned = pltpu.roll(north[k], 64, 1)
        up[k] = jnp.where(lane >= 64, south[k], turned)
        down[k] = jnp.where(lane < 64, south[k], turned)


def corners(south, north):
    vmem = pl.BlockSpec(memory_space=pltpu.VMEM)
    shape = pltpu.VMEM((9, 16, 128), f32)
    return pl.pallas_call(
        corners_body,
        in_specs=[vmem] * 2,
        out_specs=[vmem] * 2,
        out_shape=(shape, shape),
        compiler_params=pltpu.CompilerParams(vmem_limit_bytes=8 * 2**20),
        name="corners",
    )(*near(south, north))


def tendency(below, row, above, reach, spacing):
    width = row[0].shape[-1]
    square = 1.0 / (spacing * spacing)
    out = []
    for c in range(3):
        u = row[c]
        up = jnp.concatenate([u[8:16], pltpu.roll(u[0:8], 7, 0)], axis=0)
        down = jnp.concatenate([pltpu.roll(u[8:16], 1, 0), u[0:8]], axis=0)
        north = pltpu.roll(u, width - reach, 1)
        south = pltpu.roll(u, reach, 1)
        laplace = (above[c] + below[c]) + (up + down) - (4.0 + 2.0 * square) * u
        laplace = laplace + (north + south) * square
        transport = (
            row[0] * (above[c] - below[c])
            + row[1] * ((north - south) * (1.0 / spacing))
            + row[2] * (up - down)
        )
        out.append(viscosity * laplace - 0.5 * transport)
    return out


def fine_body(place, u, before, after, south, north, corner_before, corner_after,
              sources, halves_1, halves_2, ue, v1, v2, rest, f0, h1, pair_u, pair_v, native_0, native_1, turned):
    gx = place[0]
    gy = place[1]
    leader = place[2] == 0
    lane = lanes((16, 128))
    wide = lanes((16, 384))
    even = wide % 2 == 0
    low_ok = jnp.where(gx > 0, 1.0, 0.0).astype(f32)
    high_ok = jnp.where(gx < 3, 1.0, 0.0).astype(f32)
    north_ok = jnp.where(gy < 3, 1.0, 0.0).astype(f32)
    south_ok = jnp.where(gy > 0, 1.0, 0.0).astype(f32)
    columns_ok = jnp.where(wide < 256, 1.0, jnp.where(wide < 320, north_ok, south_ok))

    def gather(k, carry):
        for e in range(22):
            x = e - 3
            if x < 0:
                ue[k, e, :, 0:256] = before[k, e]
                a, b, slot_a, slot_b = corner_before, corner_before, 8 + x, 16 + x
            elif x < 16:
                ue[k, e, :, 0:128] = strided(u, k, x, 0)
                ue[k, e, :, 128:256] = strided(u, k, x, 1)
                a, b, slot_a, slot_b = north, south, x, x
            else:
                ue[k, e, :, 0:256] = after[k, x - 16]
                a, b, slot_a, slot_b = corner_after, corner_after, x - 8, x - 16
            a = a[k]
            b = b[k]
            if slot_a > 0:
                a = pltpu.roll(a, 128 - 8 * slot_a, 1)
            if slot_b < 15:
                b = pltpu.roll(b, 120 - 8 * slot_b, 1)
            ue[k, e, :, 256:384] = jnp.where(lane < 64, a, b)
        return carry

    lax.fori_loop(0, 9, gather, 0)

    def row_ok(e):
        return jnp.where(e < 3, low_ok, jnp.where(e > 18, high_ok, 1.0))

    def paired(field):
        return 0.5 * (field + jnp.where(even, pltpu.roll(field, 383, 1), pltpu.roll(field, 1, 1)))

    def first(e, carry):
        flux = []
        for node in range(3):
            rows = [[ue[3 * node + c, e + d] for c in range(3)] for d in (-1, 0, 1)]
            flux.append(tendency(*rows, 1, 1.0))
        ok = columns_ok * row_ok(e)
        for c in range(3):
            a, b, d = flux[0][c], flux[1][c], flux[2][c]
            start = ue[c, e]
            new = start + slice_step * (first_row[0] * a + first_row[1] * b + first_row[2] * d)
            new = new * ok
            v1[c, e] = new
            rest[c, e] = (
                slice_step * (second_row[0] * a + second_row[1] * b + second_row[2] * d)
                - half_step * b
            )
            f0[c, e] = a
            pair_u[c, e] = paired(start)
            pair_v[c, e] = paired(new)
        return carry

    lax.fori_loop(1, 21, first, 0)

    def second(e, carry):
        rows = [[v1[c, e + d] for c in range(3)] for d in (-1, 0, 1)]
        slope = tendency(*rows, 1, 1.0)
        ok = columns_ok * row_ok(e)
        for c in range(3):
            v2[c, e] = (rows[1][c] + half_step * slope[c] + rest[c, e]) * ok
            h1[c, e] = slope[c]
        return carry

    lax.fori_loop(2, 20, second, 0)

    def put(field, c, x, value):
        for odd in (0, 1):
            at = pl.ds((field * 3 + c) * 256 + x % 2 * 128 + x // 2 + odd * 8, 8, stride=16)
            native_0[at, :] = value[odd * 8:odd * 8 + 8, 0:128]
            native_1[at, :] = value[odd * 8:odd * 8 + 8, 128:256]

    def third(e, carry):
        rows = [[v2[c, e + d] for c in range(3)] for d in (-1, 0, 1)]
        slope = tendency(*rows, 1, 1.0)
        base_u = tendency(*[[pair_u[c, e + d] for c in range(3)] for d in (-1, 0, 1)], 2, 2.0)
        base_v = tendency(*[[pair_v[c, e + d] for c in range(3)] for d in (-1, 0, 1)], 2, 2.0)
        for c in range(3):
            a, b, d = f0[c, e], h1[c, e], slope[c]
            one = slice_step * (first_row[0] * a + first_row[1] * b + first_row[2] * d)
            two = slice_step * (second_row[0] * a + second_row[1] * b + second_row[2] * d)
            one = one + jnp.where(leader, ue[c, e], -half_step * base_u[c])
            two = two - half_step * base_v[c]
            put(0, c, e - 3, one)
            put(1, c, e - 3, two)
            put(2, c, e - 3, v1[c, e])
            put(3, c, e - 3, rows[1][c])
        return carry

    lax.fori_loop(3, 19, third, 0)

    def compact(c, carry):
        for field in range(4):
            for odd in (0, 1):
                start = pl.multiple_of((field * 3 + c) * 256 + odd * 128, 128)
                for half, native in enumerate((native_0, native_1)):
                    at = (field * 2 + odd) * 2 + half
                    turned[at] = native[pl.ds(start, 128), :].T
                    one = turned[at, pl.ds(0, 64, stride=2), :]
                    two = turned[at, pl.ds(1, 64, stride=2), :]
                    rows = pl.ds(half * 64, 64)
                    tile = pl.ds(pl.multiple_of(c * 256 + odd * 128, 128), 128)
                    if field < 2:
                        tile = pl.ds(pl.multiple_of(field * 768 + c * 256 + odd * 128, 128), 128)
                        sources[rows, tile] = 0.5 * (one + two)
                    elif field == 2:
                        halves_1[rows, tile] = 0.5 * (one - two)
                    else:
                        halves_2[rows, tile] = 0.5 * (one - two)
        return carry

    lax.fori_loop(0, 3, compact, 0)


def fine_part(place, u, *arrays):
    vmem = pl.BlockSpec(memory_space=pltpu.VMEM)
    field = pltpu.VMEM((3, 22, 16, 384), f32)
    return pl.pallas_call(
        fine_body,
        out_shape=(pltpu.VMEM((128, 1536), f32), pltpu.VMEM((128, 768), f32), pltpu.VMEM((128, 768), f32)),
        in_specs=[pl.BlockSpec(memory_space=pltpu.SMEM)] + [vmem] * (1 + len(arrays)),
        out_specs=[vmem] * 3,
        scratch_shapes=[pltpu.VMEM((9, 22, 16, 384), f32)]
        + [field] * 7
        + [pltpu.VMEM((3072, 128), f32)] * 2
        + [pltpu.VMEM((16, 128, 128), f32)],
        compiler_params=pltpu.CompilerParams(vmem_limit_bytes=36 * 2**20),
        name="fine",
    )(place, u, *near(*arrays))


def pack_body(source, to_right, to_left):
    row = lax.broadcasted_iota(jnp.int32, (8, 768), 0)
    for j in range(2):
        for field in range(2):
            k = 2 * j + field
            for xh in range(4):
                one = source[j * 4 + xh, :, field * 768:(field + 1) * 768]
                two = source[(3 - j) * 4 + xh, :, (1 - field) * 768:(2 - field) * 768]
                right = pltpu.roll(two, k, 0) if k else two
                left = pltpu.roll(two, 8 - k, 0) if k else two
                to_right[j * 4 + xh, :, field * 768:(field + 1) * 768] = jnp.where(row > k, one, right)
                to_left[j * 4 + xh, :, field * 768:(field + 1) * 768] = jnp.where(row < 7 - k, one, left)


def pack(source):
    vmem = pl.BlockSpec(memory_space=pltpu.VMEM)
    shape = pltpu.VMEM((8, 8, 1536), f32)
    return pl.pallas_call(
        pack_body,
        in_specs=[vmem],
        out_specs=[vmem] * 2,
        out_shape=(shape, shape),
        compiler_params=pltpu.CompilerParams(vmem_limit_bytes=8 * 2**20),
        name="pack",
    )(*near(source))


def stage_body(place, *rest, begins, ends):
    rest = list(rest)
    starts = () if begins else (rest.pop(0), rest.pop(0), rest.pop(0))
    source, source_left, source_right, result, buffer_0, buffer_1 = rest
    lane = lanes((24, 128))
    x_first = lane % 8 == 0
    x_last = lane % 8 == 7
    row = lax.broadcasted_iota(jnp.int32, (24, 128), 0)
    inside = ((row >= 8) | (place[3] > 0)) & ((row < 16) | (place[3] < 63))

    for c in range(3):
        for t in range(8):
            for buffer in (buffer_0, buffer_1):
                buffer[c, t, 0:8] = jnp.zeros((8, 128), f32)
                buffer[c, t, 32:40] = jnp.zeros((8, 128), f32)
            if begins:
                buffer_0[c, t, 8:32] = jnp.zeros((24, 128), f32)
            else:
                own, left, right = starts
                buffer_0[c, t, 8:16] = left[c, t]
                buffer_0[c, t, 16:24] = own[c, t]
                buffer_0[c, t, 24:32] = right[c, t]

    def keep(j, field, buffer):
        for xh in range(4):
            for c in range(3):
                for odd in range(2):
                    at = (field * 6 + c * 2 + odd) * 128
                    result[j * 4 + xh, :, at:at + 128] = buffer[c, xh * 2 + odd, 16:24]

    square = 0.25
    c_side = half_step * viscosity
    c_second = half_step * viscosity * square
    c_centre = 1.0 - half_step * viscosity * (4.0 + 2.0 * square)

    def step(j, field, old, new, late):
        k = 2 * j + field
        for xh in range(4):
            for odd in range(2):
                t = 2 * xh + odd
                u = [old[c, t, 8:32] for c in range(3)]
                k0 = u[0] * (-0.5 * half_step)
                k1 = u[1] * (-0.25 * half_step)
                k2 = u[2] * (-0.5 * half_step)
                for c in range(3):
                    v = u[c]
                    other = old[c, t + 1 - 2 * odd, 8:32]
                    if odd:
                        beyond = pltpu.roll(old[c, t + 1, 8:32], 7, 1) if xh < 3 else 0.0
                        east = jnp.where(x_last, beyond, pltpu.roll(other, 127, 1))
                        west = other
                    else:
                        beyond = pltpu.roll(old[c, t - 1, 8:32], 121, 1) if xh > 0 else 0.0
                        east = other
                        west = jnp.where(x_first, beyond, pltpu.roll(other, 1, 1))
                    up = pltpu.roll(v, 120, 1)
                    down = pltpu.roll(v, 8, 1)
                    north = old[c, t, 9:33]
                    south = old[c, t, 7:31]
                    at = (field * 6 + c * 2 + odd) * 128
                    if late:
                        there = ((1 - field) * 6 + c * 2 + odd) * 128
                        pull_left = pltpu.roll(source_left[(3 - j) * 4 + xh, :, there:there + 128], (1 + k) % 8, 0)
                        pull_right = pltpu.roll(source_right[(3 - j) * 4 + xh, :, there:there + 128], 7 - k, 0)
                    else:
                        pull_left = source_left[j * 4 + xh, :, at:at + 128]
                        pull_right = source_right[j * 4 + xh, :, at:at + 128]
                    pull = jnp.concatenate(
                        [pull_left, source[j * 4 + xh, :, at:at + 128], pull_right], axis=0
                    )
                    value = (
                        c_centre * v
                        + c_side * ((east + west) + (up + down))
                        + c_second * (north + south)
                        + (k0 * (east - west) + k1 * (north - south) + k2 * (up - down))
                        + pull
                    )
                    new[c, t, 8:32] = jnp.where(inside, value, 0.0)

    def one_slice(j, late):
        if ends:
            keep(j, 0, buffer_0)
        step(j, 0, buffer_0, buffer_1, late)
        if ends:
            keep(j, 1, buffer_1)
        step(j, 1, buffer_1, buffer_0, late)
        if ends:
            keep(j, 2, buffer_0)

    def early(j, carry):
        one_slice(j, False)
        return carry

    def later(j, carry):
        one_slice(j, True)
        return carry

    lax.fori_loop(0, 2, early, 0)
    lax.fori_loop(2, 4, later, 0)
    if not ends:
        for c in range(3):
            for t in range(8):
                result[c, t] = buffer_0[c, t, 16:24]


def stage(place, starts, sources, ends):
    vmem = pl.BlockSpec(memory_space=pltpu.VMEM)
    arrays = near(*starts, *sources)
    return pl.pallas_call(
        functools.partial(stage_body, begins=not starts, ends=ends),
        out_shape=pltpu.VMEM((16, 8, 2304) if ends else (3, 8, 8, 128), f32),
        in_specs=[pl.BlockSpec(memory_space=pltpu.SMEM)] + [vmem] * len(arrays),
        out_specs=vmem,
        scratch_shapes=[pltpu.VMEM((3, 8, 40, 128), f32)] * 2,
        compiler_params=pltpu.CompilerParams(vmem_limit_bytes=12 * 2**20),
        name="stage",
    )(place, *arrays)


def finish_body(place, start, coarse, halves_0, halves_1, halves_2, out, mixed, rows):
    for field, halves in enumerate((halves_0, halves_1, halves_2)):
        def each(c, carry):
            for half in range(2):
                part = pl.ds(half * 64, 64)
                for odd in range(2):
                    tile = pl.multiple_of(c * 256 + odd * 128, 128)
                    w = coarse[part, pl.ds(field * 768 + tile, 128)]
                    e = halves[part, pl.ds(tile, 128)]
                    at = half * 2 + odd
                    mixed[at, pl.ds(0, 64, stride=2), :] = w + e
                    mixed[at, pl.ds(1, 64, stride=2), :] = w - e
                    rows[half, pl.ds(odd, 128, stride=2), :] = mixed[at].T
                out[pl.ds((field * 3 + c) * 32, 32), half] = rows[half].reshape(32, 8, 128)
            return carry

        lax.fori_loop(0, 3, each, 0)

    @pl.when(place[2] == 0)
    def _():
        pltpu.sync_copy(start.at[pl.ds(0, 96)], out.at[pl.ds(0, 96)])


def finish(place, start, coarse, *halves):
    vmem = pl.BlockSpec(memory_space=pltpu.VMEM)
    return pl.pallas_call(
        finish_body,
        out_shape=jax.ShapeDtypeStruct((288, 2, 8, 128), f32),
        in_specs=[pl.BlockSpec(memory_space=pltpu.SMEM), pl.BlockSpec(memory_space=pl.ANY)] + [vmem] * 4,
        scratch_shapes=[pltpu.VMEM((4, 128, 128), f32), pltpu.VMEM((2, 256, 128), f32)],
        compiler_params=pltpu.CompilerParams(vmem_limit_bytes=16 * 2**20),
        name="finish",
    )(place, start, *near(coarse, *halves))


def sent(block, axes, sizes, moves):
    strides = {}
    total = 1
    for axis in reversed(axes):
        strides[axis] = total
        total *= sizes[axis]
    pairs = []
    for source in range(total):
        target = source
        for axis, by in moves.items():
            at = source // strides[axis] % sizes[axis]
            if not 0 <= at + by < sizes[axis]:
                target = None
                break
            target += by * strides[axis]
        if target is not None:
            pairs.append((source, target))
    return lax.ppermute(block, axes if len(axes) > 1 else axes[0], pairs)


def solution(mesh):
    sizes = {"tz": 4, "ty": 4, "gx": 4, "gy": 4}
    fine_mesh = Mesh(mesh.devices.reshape(4, 4, 4, 4), tuple(sizes))
    pieces = ("ty", "gx", "gy")

    def beside(block, by):
        name = lambda piece: (piece % 16) * 4 + piece // 16
        pairs = [(name(i), name(i + by)) for i in range(64) if 0 <= i + by < 64]
        return lax.ppermute(block, pieces, pairs)

    def per_device(provisional):
        tz, ty, gx, gy = (lax.axis_index(a) for a in sizes)
        place = jnp.stack([gx, gy, tz * 4 + ty, gy * 16 + ty * 4 + gx]).astype(jnp.int32)
        tiles = provisional.reshape(288, 8, 2, 128).transpose(0, 2, 1, 3)
        u = tiles.reshape(4608, 128)
        low_rows, high_rows, low_columns, high_columns = edges(u)
        after = sent(low_rows, ("gx",), sizes, {"gx": -1})
        before = sent(high_rows, ("gx",), sizes, {"gx": 1})
        south = sent(high_columns, ("gy",), sizes, {"gy": 1})
        north = sent(low_columns, ("gy",), sizes, {"gy": -1})
        up, down = corners(south, north)
        corner_before = sent(up, ("gx",), sizes, {"gx": 1})
        corner_after = sent(down, ("gx",), sizes, {"gx": -1})
        sources, halves_1, halves_2 = fine_part(
            place, u, before, after, south, north, corner_before, corner_after
        )
        halves_0 = lax.ppermute(halves_2, ("tz", "ty"), [(i, i + 1) for i in range(15)])
        source = lax.all_to_all(sources.reshape(16, 8, 1536), group_axes, 0, 0)
        to_right, to_left = pack(source)
        source_left = beside(to_right, 1)
        source_right = beside(to_left, -1)
        starts = ()
        for turn in range(4):
            own = stage(place, starts, (source, source_left, source_right), turn == 3)
            if turn < 3:
                own = sent(own, ("tz",), sizes, {"tz": 1})
                starts = (own, beside(own, 1), beside(own, -1))
        coarse = lax.all_to_all(own, group_axes, 0, 0).reshape(128, 2304)
        out = finish(place, tiles, coarse, halves_0, halves_1, halves_2)
        return out.transpose(0, 2, 1, 3).reshape(1, 3, 3, 16, 16, 256)

    spec = P(("tz", "ty"), None, None, None, "gx", "gy")

    return jax.shard_map(per_device, mesh=fine_mesh, in_specs=(spec,), out_specs=spec, check_vma=False)
```

```python
import functools

import jax
import jax.numpy as jnp
from jax import lax
from jax.experimental import pallas as pl
from jax.experimental.pallas import tpu as pltpu
from jax.sharding import Mesh
from jax.sharding import PartitionSpec as P


viscosity = 0.1
slice_step = 0.25
half_step = 0.125
first_row = (5.0 / 24.0, 1.0 / 3.0, -1.0 / 24.0)
second_row = (-1.0 / 24.0, 1.0 / 3.0, 5.0 / 24.0)

f32 = jnp.float32
group_axes = ("ty", "gx")


def snake(piece):
    return piece if piece // 4 % 2 == 0 else piece // 4 * 4 + 3 - piece % 4


def device_of(piece, gy):
    return jnp.where(gy % 2 == 0, snake(piece), snake(15 - piece))


def near(*arrays):
    return tuple(pltpu.with_memory_space_constraint(a, pltpu.VMEM) for a in arrays)


def lanes(shape):
    return lax.broadcasted_iota(jnp.int32, shape, len(shape) - 1)


def strided(u, k, x, half):
    at = k * 512 + x // 8 * 16 + half * 8 + x % 8
    return jnp.concatenate([u[pl.ds(at + 32 * odd, 8, stride=64), :] for odd in (0, 1)], axis=0)


def edges_body(u, field, low_rows, high_rows, held, arrived):
    copies = [pltpu.make_async_copy(u.at[pl.ds(512 * k, 512)], held.at[pl.ds(512 * k, 512)], arrived.at[k]) for k in range(9)]
    for copy in copies:
        copy.start()
    for k in range(9):
        copies[k].wait()
        for x in range(16):
            for half in range(2):
                at = pl.ds(half * 128, 128)
                row = strided(held, k, x, half)
                field[k, x, :, at] = row
                if x < 3:
                    low_rows[k, x, :, at] = row
                if x > 12:
                    high_rows[k, x - 13, :, at] = row


def edges(u):
    vmem = pl.BlockSpec(memory_space=pltpu.VMEM)
    rows = pltpu.VMEM((9, 3, 16, 256), f32)
    return pl.pallas_call(
        edges_body,
        in_specs=[pl.BlockSpec(memory_space=pltpu.HBM)],
        out_specs=[vmem] * 3,
        out_shape=(pltpu.VMEM((9, 16, 16, 256), f32), rows, rows),
        scratch_shapes=[pltpu.VMEM((4608, 128), f32), pltpu.SemaphoreType.DMA((9,))],
        compiler_params=pltpu.CompilerParams(vmem_limit_bytes=12 * 2**20),
        name="edges",
    )(pltpu.with_memory_space_constraint(u, pltpu.HBM))


def columns_body(field, before, after, low_columns, high_columns):
    slot = lanes((16, 128)) // 4

    def each(k, carry):
        left = jnp.zeros((16, 128), f32)
        right = jnp.zeros((16, 128), f32)
        for e in range(22):
            ref, x = (before, e) if e < 3 else (field, e - 3) if e < 19 else (after, e - 19)
            a = ref[k, x, :, 0:128]
            b = ref[k, x, :, 128:256]
            left = jnp.where(slot == e, pltpu.roll(a, 4 * e, 1) if e else a, left)
            right = jnp.where(slot == e, pltpu.roll(b, 4 * e + 4, 1), right)
        low_columns[k] = left
        high_columns[k] = right
        return carry

    lax.fori_loop(0, 9, each, 0)


def columns(field, before, after):
    vmem = pl.BlockSpec(memory_space=pltpu.VMEM)
    shape = pltpu.VMEM((9, 16, 128), f32)
    return pl.pallas_call(
        columns_body,
        in_specs=[vmem] * 3,
        out_specs=[vmem] * 2,
        out_shape=(shape, shape),
        compiler_params=pltpu.CompilerParams(vmem_limit_bytes=8 * 2**20),
        name="columns",
    )(*near(field, before, after))


def tendency(below, row, above, reach, spacing):
    width = row[0].shape[-1]
    square = 1.0 / (spacing * spacing)
    out = []
    for c in range(3):
        u = row[c]
        up = jnp.concatenate([u[8:16], pltpu.roll(u[0:8], 7, 0)], axis=0)
        down = jnp.concatenate([pltpu.roll(u[8:16], 1, 0), u[0:8]], axis=0)
        north = pltpu.roll(u, width - reach, 1)
        south = pltpu.roll(u, reach, 1)
        laplace = (above[c] + below[c]) + (up + down) - (4.0 + 2.0 * square) * u
        laplace = laplace + (north + south) * square
        transport = (
            row[0] * (above[c] - below[c])
            + row[1] * ((north - south) * (1.0 / spacing))
            + row[2] * (up - down)
        )
        out.append((2.0 * viscosity) * laplace - transport)
    return out


def fine_body(place, field, before, after, south, north,
              sources, halves_1, halves_2, ue, v1, v2, rest, f0, h1, pair_u, pair_v, native_0, native_1, turned):
    gx = place[0]
    gy = place[1]
    quarter = 0.5 * slice_step
    one_0, one_1, one_2 = (quarter * w for w in first_row)
    two_0, two_1, two_2 = (quarter * w for w in second_row)
    leader = place[2] == 0
    lane = lanes((16, 128))
    wide = lanes((16, 384))
    even = wide % 2 == 0
    low_ok = jnp.where(gx > 0, 1.0, 0.0).astype(f32)
    high_ok = jnp.where(gx < 3, 1.0, 0.0).astype(f32)
    north_ok = jnp.where(gy < 3, 1.0, 0.0).astype(f32)
    south_ok = jnp.where(gy > 0, 1.0, 0.0).astype(f32)
    columns_ok = jnp.where(wide < 256, 1.0, jnp.where(wide < 320, north_ok, south_ok))

    def gather(k, carry):
        a = north[k]
        b = south[k]
        for e in range(22):
            ref, x = (before, e) if e < 3 else (field, e - 3) if e < 19 else (after, e - 19)
            ue[k, e, :, 0:256] = ref[k, x]
            right = pltpu.roll(a, 128 - 4 * e, 1) if e else a
            ue[k, e, :, 256:384] = jnp.where(lane < 64, right, pltpu.roll(b, 124 - 4 * e, 1))
        return carry

    lax.fori_loop(0, 9, gather, 0)

    def row_ok(e):
        return jnp.where(e < 3, low_ok, jnp.where(e > 18, high_ok, 1.0))

    def paired(field):
        return 0.5 * (field + jnp.where(even, pltpu.roll(field, 383, 1), pltpu.roll(field, 1, 1)))

    def first(e, carry):
        flux = []
        for node in range(3):
            rows = [[ue[3 * node + c, e + d] for c in range(3)] for d in (-1, 0, 1)]
            flux.append(tendency(*rows, 1, 1.0))
        ok = columns_ok * row_ok(e)
        for c in range(3):
            a, b, d = flux[0][c], flux[1][c], flux[2][c]
            start = ue[c, e]
            new = (start + (one_0 * a + one_1 * b + one_2 * d)) * ok
            v1[c, e] = new
            rest[c, e] = two_0 * a + (two_1 - 0.5 * half_step) * b + two_2 * d
            f0[c, e] = a
            pair_u[c, e] = paired(start)
            pair_v[c, e] = paired(new)
        return carry

    lax.fori_loop(1, 21, first, 0)

    def second(e, carry):
        rows = [[v1[c, e + d] for c in range(3)] for d in (-1, 0, 1)]
        slope = tendency(*rows, 1, 1.0)
        ok = columns_ok * row_ok(e)
        for c in range(3):
            v2[c, e] = (rows[1][c] + (0.5 * half_step) * slope[c] + rest[c, e]) * ok
            h1[c, e] = slope[c]
        return carry

    lax.fori_loop(2, 20, second, 0)

    def put(field, c, x, value):
        for odd in (0, 1):
            at = pl.ds((field * 3 + c) * 256 + x % 2 * 128 + x // 2 + odd * 8, 8, stride=16)
            native_0[at, :] = value[odd * 8:odd * 8 + 8, 0:128]
            native_1[at, :] = value[odd * 8:odd * 8 + 8, 128:256]

    def third(e, carry):
        rows = [[v2[c, e + d] for c in range(3)] for d in (-1, 0, 1)]
        slope = tendency(*rows, 1, 1.0)
        base_u = tendency(*[[pair_u[c, e + d] for c in range(3)] for d in (-1, 0, 1)], 2, 2.0)
        base_v = tendency(*[[pair_v[c, e + d] for c in range(3)] for d in (-1, 0, 1)], 2, 2.0)
        for c in range(3):
            a, b, d = f0[c, e], h1[c, e], slope[c]
            one = one_0 * a + one_1 * b + one_2 * d
            two = two_0 * a + two_1 * b + two_2 * d
            one = one + jnp.where(leader, ue[c, e], (-0.5 * half_step) * base_u[c])
            two = two - (0.5 * half_step) * base_v[c]
            put(0, c, e - 3, one)
            put(1, c, e - 3, two)
            put(2, c, e - 3, v1[c, e])
            put(3, c, e - 3, rows[1][c])
        return carry

    lax.fori_loop(3, 19, third, 0)

    def compact(c, carry):
        for field in range(4):
            for odd in (0, 1):
                start = pl.multiple_of((field * 3 + c) * 256 + odd * 128, 128)
                for half, native in enumerate((native_0, native_1)):
                    at = (field * 2 + odd) * 2 + half
                    turned[at] = native[pl.ds(start, 128), :].T
                    one = turned[at, pl.ds(0, 64, stride=2), :]
                    two = turned[at, pl.ds(1, 64, stride=2), :]
                    rows = pl.ds(half * 64, 64)
                    tile = pl.ds(pl.multiple_of(c * 256 + odd * 128, 128), 128)
                    if field < 2:
                        tile = pl.ds(pl.multiple_of(field * 768 + c * 256 + odd * 128, 128), 128)
                        mean = 0.5 * (one + two)
                        for i in range(8):
                            sources[device_of(half * 8 + i, gy), :, tile] = mean[8 * i:8 * i + 8]
                    elif field == 2:
                        halves_1[rows, tile] = 0.5 * (one - two)
                    else:
                        halves_2[rows, tile] = 0.5 * (one - two)
        return carry

    lax.fori_loop(0, 3, compact, 0)


def fine_part(place, *arrays):
    vmem = pl.BlockSpec(memory_space=pltpu.VMEM)
    field = pltpu.VMEM((3, 22, 16, 384), f32)
    return pl.pallas_call(
        fine_body,
        out_shape=(
            pltpu.VMEM((16, 8, 1536), f32),
            jax.ShapeDtypeStruct((128, 768), f32),
            pltpu.VMEM((128, 768), f32),
        ),
        in_specs=[pl.BlockSpec(memory_space=pltpu.SMEM)] + [vmem] * len(arrays),
        out_specs=[vmem] * 3,
        scratch_shapes=[pltpu.VMEM((9, 22, 16, 384), f32)]
        + [field] * 7
        + [pltpu.VMEM((3072, 128), f32)] * 2
        + [pltpu.VMEM((16, 128, 128), f32)],
        compiler_params=pltpu.CompilerParams(vmem_limit_bytes=36 * 2**20),
        name="fine",
    )(place, *near(*arrays))


def pack_body(source, to_right, to_left):
    row = lax.broadcasted_iota(jnp.int32, (8, 768), 0)
    for j in range(2):
        for field in range(2):
            k = 2 * j + field
            for xh in range(4):
                one = source[j * 4 + xh, :, field * 768:(field + 1) * 768]
                two = source[(3 - j) * 4 + xh, :, (1 - field) * 768:(2 - field) * 768]
                right = pltpu.roll(two, k, 0) if k else two
                left = pltpu.roll(two, 8 - k, 0) if k else two
                to_right[j * 4 + xh, :, field * 768:(field + 1) * 768] = jnp.where(row > k, one, right)
                to_left[j * 4 + xh, :, field * 768:(field + 1) * 768] = jnp.where(row < 7 - k, one, left)


def pack(source):
    vmem = pl.BlockSpec(memory_space=pltpu.VMEM)
    shape = pltpu.VMEM((8, 8, 1536), f32)
    return pl.pallas_call(
        pack_body,
        in_specs=[vmem],
        out_specs=[vmem] * 2,
        out_shape=(shape, shape),
        compiler_params=pltpu.CompilerParams(vmem_limit_bytes=8 * 2**20),
        name="pack",
    )(*near(source))


def stage_body(place, *rest, begins, ends):
    rest = list(rest)
    starts = () if begins else (rest.pop(0), rest.pop(0), rest.pop(0))
    source, source_left, source_right, result, buffer_0, buffer_1 = rest
    lane = lanes((24, 128))
    x_first = lane % 8 == 0
    x_last = lane % 8 == 7
    row = lax.broadcasted_iota(jnp.int32, (24, 128), 0)
    inside = ((row >= 8) | (place[3] > 0)) & ((row < 16) | (place[3] < 63))

    for c in range(3):
        for t in range(8):
            for buffer in (buffer_0, buffer_1):
                buffer[c, t, 0:8] = jnp.zeros((8, 128), f32)
                buffer[c, t, 32:40] = jnp.zeros((8, 128), f32)
            if begins:
                buffer_0[c, t, 8:32] = jnp.zeros((24, 128), f32)
            else:
                own, left, right = starts
                buffer_0[c, t, 8:16] = left[c, t]
                buffer_0[c, t, 16:24] = own[c, t]
                buffer_0[c, t, 24:32] = right[c, t]

    def keep(j, field, buffer):
        for xh in range(4):
            for c in range(3):
                for odd in range(2):
                    at = (field * 6 + c * 2 + odd) * 128
                    result[j * 4 + xh, :, at:at + 128] = buffer[c, xh * 2 + odd, 16:24]

    square = 0.25
    c_side = half_step * viscosity
    c_second = half_step * viscosity * square
    c_centre = 1.0 - half_step * viscosity * (4.0 + 2.0 * square)

    def step(j, field, old, new, late):
        k = 2 * j + field
        for xh in range(4):
            for odd in range(2):
                t = 2 * xh + odd
                u = [old[c, t, 8:32] for c in range(3)]
                k0 = u[0] * (-0.5 * half_step)
                k1 = u[1] * (-0.25 * half_step)
                k2 = u[2] * (-0.5 * half_step)
                for c in range(3):
                    v = u[c]
                    other = old[c, t + 1 - 2 * odd, 8:32]
                    if odd:
                        beyond = pltpu.roll(old[c, t + 1, 8:32], 7, 1) if xh < 3 else 0.0
                        east = jnp.where(x_last, beyond, pltpu.roll(other, 127, 1))
                        west = other
                    else:
                        beyond = pltpu.roll(old[c, t - 1, 8:32], 121, 1) if xh > 0 else 0.0
                        east = other
                        west = jnp.where(x_first, beyond, pltpu.roll(other, 1, 1))
                    up = pltpu.roll(v, 120, 1)
                    down = pltpu.roll(v, 8, 1)
                    north = old[c, t, 9:33]
                    south = old[c, t, 7:31]
                    at = (field * 6 + c * 2 + odd) * 128
                    if late:
                        there = ((1 - field) * 6 + c * 2 + odd) * 128
                        pull_left = pltpu.roll(source_left[(3 - j) * 4 + xh, :, there:there + 128], (1 + k) % 8, 0)
                        pull_right = pltpu.roll(source_right[(3 - j) * 4 + xh, :, there:there + 128], 7 - k, 0)
                    else:
                        pull_left = source_left[j * 4 + xh, :, at:at + 128]
                        pull_right = source_right[j * 4 + xh, :, at:at + 128]
                    pull = jnp.concatenate(
                        [pull_left, source[j * 4 + xh, :, at:at + 128], pull_right], axis=0
                    )
                    value = (
                        c_centre * v
                        + c_side * ((east + west) + (up + down))
                        + c_second * (north + south)
                        + (k0 * (east - west) + k1 * (north - south) + k2 * (up - down))
                        + pull
                    )
                    new[c, t, 8:32] = jnp.where(inside, value, 0.0)

    def one_slice(j, late):
        if ends:
            keep(j, 0, buffer_0)
        step(j, 0, buffer_0, buffer_1, late)
        if ends:
            keep(j, 1, buffer_1)
        step(j, 1, buffer_1, buffer_0, late)
        if ends:
            keep(j, 2, buffer_0)

    def early(j, carry):
        one_slice(j, False)
        return carry

    def later(j, carry):
        one_slice(j, True)
        return carry

    lax.fori_loop(0, 2, early, 0)
    lax.fori_loop(2, 4, later, 0)
    if not ends:
        for c in range(3):
            for t in range(8):
                result[c, t] = buffer_0[c, t, 16:24]


def stage(place, starts, sources, ends):
    vmem = pl.BlockSpec(memory_space=pltpu.VMEM)
    arrays = near(*starts, *sources)
    return pl.pallas_call(
        functools.partial(stage_body, begins=not starts, ends=ends),
        out_shape=pltpu.VMEM((16, 8, 2304) if ends else (3, 8, 8, 128), f32),
        in_specs=[pl.BlockSpec(memory_space=pltpu.SMEM)] + [vmem] * len(arrays),
        out_specs=vmem,
        scratch_shapes=[pltpu.VMEM((3, 8, 40, 128), f32)] * 2,
        compiler_params=pltpu.CompilerParams(vmem_limit_bytes=12 * 2**20),
        name="stage",
    )(place, *arrays)


def finish_body(place, start, coarse, halves_0, halves_1, halves_2, out, mixed, rows):
    gy = place[1]

    def one_field(field, halves):
        for c in range(3):
            for half in range(2):
                for odd in range(2):
                    tile = pl.ds(field * 768 + c * 256 + odd * 128, 128)
                    w = jnp.concatenate(
                        [coarse[device_of(half * 8 + i, gy), :, tile] for i in range(8)], axis=0
                    )
                    e = halves[pl.ds(half * 64, 64), pl.ds(c * 256 + odd * 128, 128)]
                    at = (c * 2 + half) * 2 + odd
                    mixed[at, pl.ds(0, 64, stride=2), :] = w + e
                    mixed[at, pl.ds(1, 64, stride=2), :] = w - e
                    rows[c * 2 + half, pl.ds(odd, 128, stride=2), :] = mixed[at].T
                out[pl.ds(c * 32, 32), half] = rows[c * 2 + half].reshape(32, 8, 128)

    for field, halves in enumerate((halves_0, halves_1, halves_2)):
        if field:
            chosen = pl.program_id(0) == field
        else:
            chosen = (pl.program_id(0) == 0) & (place[2] > 0)
        pl.when(chosen)(functools.partial(one_field, field, halves))

    @pl.when((pl.program_id(0) == 0) & (place[2] == 0))
    def _():
        pltpu.sync_copy(start.at[pl.ds(0, 96)], out)


def finish(place, start, coarse, *halves):
    vmem = pl.BlockSpec(memory_space=pltpu.VMEM)
    return pl.pallas_call(
        finish_body,
        grid=(3,),
        out_shape=jax.ShapeDtypeStruct((288, 2, 8, 128), f32),
        in_specs=[pl.BlockSpec(memory_space=pltpu.SMEM), pl.BlockSpec(memory_space=pl.ANY)] + [vmem] * 4,
        out_specs=pl.BlockSpec((96, 2, 8, 128), lambda f: (f, 0, 0, 0)),
        scratch_shapes=[pltpu.VMEM((12, 128, 128), f32), pltpu.VMEM((6, 256, 128), f32)],
        compiler_params=pltpu.CompilerParams(vmem_limit_bytes=16 * 2**20),
        name="finish",
    )(place, start, *near(coarse), *halves)


def sent(block, axes, sizes, moves):
    strides = {}
    total = 1
    for axis in reversed(axes):
        strides[axis] = total
        total *= sizes[axis]
    pairs = []
    for source in range(total):
        target = source
        for axis, by in moves.items():
            at = source // strides[axis] % sizes[axis]
            if not 0 <= at + by < sizes[axis]:
                target = None
                break
            target += by * strides[axis]
        if target is not None:
            pairs.append((source, target))
    return lax.ppermute(block, axes if len(axes) > 1 else axes[0], pairs)


def solution(mesh):
    sizes = {"tz": 4, "ty": 4, "gx": 4, "gy": 4}
    fine_mesh = Mesh(mesh.devices.reshape(4, 4, 4, 4), tuple(sizes))
    pieces = ("ty", "gx", "gy")

    def beside(block, by):
        def name(piece):
            gy, at = divmod(piece, 16)
            return snake(15 - at if gy % 2 else at) * 4 + gy

        pairs = [(name(i), name(i + by)) for i in range(64) if 0 <= i + by < 64]
        return lax.ppermute(block, pieces, pairs)

    def per_device(provisional):
        tz, ty, gx, gy = (lax.axis_index(a) for a in sizes)
        piece = ty * 4 + jnp.where(ty % 2 == 0, gx, 3 - gx)
        piece = gy * 16 + jnp.where(gy % 2 == 0, piece, 15 - piece)
        place = jnp.stack([gx, gy, tz * 4 + ty, piece]).astype(jnp.int32)
        tiles = provisional.reshape(288, 8, 2, 128).transpose(0, 2, 1, 3)
        field, low_rows, high_rows = edges(tiles.reshape(4608, 128))
        after = sent(low_rows, ("gx",), sizes, {"gx": -1})
        before = sent(high_rows, ("gx",), sizes, {"gx": 1})
        low_columns, high_columns = columns(field, before, after)
        south = sent(high_columns, ("gy",), sizes, {"gy": 1})
        north = sent(low_columns, ("gy",), sizes, {"gy": -1})
        sources, halves_1, halves_2 = fine_part(place, field, before, after, south, north)
        halves_0 = lax.ppermute(halves_2, ("tz", "ty"), [(i, i + 1) for i in range(15)])
        source = lax.all_to_all(sources, group_axes, 0, 0)
        to_right, to_left = pack(source)
        source_left = beside(to_right, 1)
        source_right = beside(to_left, -1)
        starts = ()
        for turn in range(4):
            own = stage(place, starts, (source, source_left, source_right), turn == 3)
            if turn < 3:
                own = sent(own, ("tz",), sizes, {"tz": 1})
                starts = (own, beside(own, 1), beside(own, -1))
            if turn == 2:
                starts, halves_0 = lax.optimization_barrier((starts, halves_0))
        coarse = lax.all_to_all(own, group_axes, 0, 0)
        out = finish(place, tiles, coarse, halves_0, halves_1, halves_2)
        return out.transpose(0, 2, 1, 3).reshape(1, 3, 3, 16, 16, 256)

    spec = P(("tz", "ty"), None, None, None, "gx", "gy")

    return jax.shard_map(per_device, mesh=fine_mesh, in_specs=(spec,), out_specs=spec, check_vma=False)
```

```python
import functools

import jax
import jax.numpy as jnp
from jax import lax
from jax.experimental import pallas as pl
from jax.experimental.pallas import tpu as pltpu
from jax.sharding import Mesh
from jax.sharding import PartitionSpec as P


viscosity = 0.1
slice_step = 0.25
half_step = 0.125
first_row = (5.0 / 24.0, 1.0 / 3.0, -1.0 / 24.0)
second_row = (-1.0 / 24.0, 1.0 / 3.0, 5.0 / 24.0)

f32 = jnp.float32
group_axes = ("ty", "gx")


def snake(piece):
    return piece if piece // 4 % 2 == 0 else piece // 4 * 4 + 3 - piece % 4


def device_of(piece, gy):
    return jnp.where(gy % 2 == 0, snake(piece), snake(15 - piece))


def near(*arrays):
    return tuple(pltpu.with_memory_space_constraint(a, pltpu.VMEM) for a in arrays)


def lanes(shape):
    return lax.broadcasted_iota(jnp.int32, shape, len(shape) - 1)


def strided(u, k, x, half):
    at = k * 512 + x // 8 * 16 + half * 8 + x % 8
    return jnp.concatenate([u[pl.ds(at + 32 * odd, 8, stride=64), :] for odd in (0, 1)], axis=0)


def edges_body(u, held, low_rows, high_rows, arrived):
    copies = [
        pltpu.make_async_copy(u.at[pl.ds(512 * k, 512)], held.at[pl.ds(512 * k, 512)], arrived.at[k])
        for k in range(9)
    ]
    for copy in copies:
        copy.start()
    for k in range(9):
        copies[k].wait()
        for x in (0, 1, 2, 13, 14, 15):
            to = low_rows.at[k, x] if x < 3 else high_rows.at[k, x - 13]
            for half in range(2):
                to[:, half * 128:(half + 1) * 128] = strided(held, k, x, half)


def edges(u):
    vmem = pl.BlockSpec(memory_space=pltpu.VMEM)
    rows = pltpu.VMEM((9, 3, 16, 256), f32)
    return pl.pallas_call(
        edges_body,
        in_specs=[pl.BlockSpec(memory_space=pltpu.HBM)],
        out_specs=[vmem] * 3,
        out_shape=(pltpu.VMEM((4608, 128), f32), rows, rows),
        scratch_shapes=[pltpu.SemaphoreType.DMA((9,))],
        compiler_params=pltpu.CompilerParams(vmem_limit_bytes=12 * 2**20),
        name="edges",
    )(pltpu.with_memory_space_constraint(u, pltpu.HBM))


def turned_body(held, field):
    def each(k, carry):
        for x in range(16):
            for half in range(2):
                field[k, x, :, half * 128:(half + 1) * 128] = strided(held, k, x, half)
        return carry

    lax.fori_loop(0, 9, each, 0)


def turned_field(held):
    vmem = pl.BlockSpec(memory_space=pltpu.VMEM)
    return pl.pallas_call(
        turned_body,
        in_specs=[vmem],
        out_specs=vmem,
        out_shape=pltpu.VMEM((9, 16, 16, 256), f32),
        compiler_params=pltpu.CompilerParams(vmem_limit_bytes=8 * 2**20),
        name="turned",
    )(*near(held))


def columns_body(field, before, after, low_columns, high_columns):
    slot = lanes((16, 128)) // 4

    def each(k, carry):
        left = jnp.zeros((16, 128), f32)
        right = jnp.zeros((16, 128), f32)
        for e in range(22):
            ref, x = (before, e) if e < 3 else (field, e - 3) if e < 19 else (after, e - 19)
            a = ref[k, x, :, 0:128]
            b = ref[k, x, :, 128:256]
            left = jnp.where(slot == e, pltpu.roll(a, 4 * e, 1) if e else a, left)
            right = jnp.where(slot == e, pltpu.roll(b, 4 * e + 4, 1), right)
        low_columns[k] = left
        high_columns[k] = right
        return carry

    lax.fori_loop(0, 9, each, 0)


def columns(field, before, after):
    vmem = pl.BlockSpec(memory_space=pltpu.VMEM)
    shape = pltpu.VMEM((9, 16, 128), f32)
    return pl.pallas_call(
        columns_body,
        in_specs=[vmem] * 3,
        out_specs=[vmem] * 2,
        out_shape=(shape, shape),
        compiler_params=pltpu.CompilerParams(vmem_limit_bytes=8 * 2**20),
        name="columns",
    )(*near(field, before, after))


def tendency(below, row, above, reach, spacing):
    width = row[0].shape[-1]
    square = 1.0 / (spacing * spacing)
    out = []
    for c in range(3):
        u = row[c]
        up = jnp.concatenate([u[8:16], pltpu.roll(u[0:8], 7, 0)], axis=0)
        down = jnp.concatenate([pltpu.roll(u[8:16], 1, 0), u[0:8]], axis=0)
        north = pltpu.roll(u, width - reach, 1)
        south = pltpu.roll(u, reach, 1)
        laplace = (above[c] + below[c]) + (up + down) - (4.0 + 2.0 * square) * u
        laplace = laplace + (north + south) * square
        transport = (
            row[0] * (above[c] - below[c])
            + row[1] * ((north - south) * (1.0 / spacing))
            + row[2] * (up - down)
        )
        out.append((2.0 * viscosity) * laplace - transport)
    return out


quarter = 0.5 * slice_step
one_0, one_1, one_2 = (quarter * w for w in first_row)
two_0, two_1, two_2 = (quarter * w for w in second_row)


def put(natives, base, x, value):
    for odd in (0, 1):
        at = pl.ds(base + x % 2 * 128 + x // 2 + odd * 8, 8, stride=16)
        for half, native in enumerate(natives):
            native[at, :] = value[odd * 8:odd * 8 + 8, half * 128:(half + 1) * 128]


def split_pairs(native, start, scratch):
    scratch[...] = native[pl.ds(start, 128), :].T
    return scratch[pl.ds(0, 64, stride=2), :], scratch[pl.ds(1, 64, stride=2), :]


def fine_body(place, field, before, after, south, north,
              halves_2, v1, v2, f0, h1, pair_u, pair_v, ue, rest, native_0, native_1, turned):
    gx = place[0]
    gy = place[1]
    lane = lanes((16, 128))
    wide = lanes((16, 384))
    even = wide % 2 == 0
    low_ok = jnp.where(gx > 0, 1.0, 0.0).astype(f32)
    high_ok = jnp.where(gx < 3, 1.0, 0.0).astype(f32)
    north_ok = jnp.where(gy < 3, 1.0, 0.0).astype(f32)
    south_ok = jnp.where(gy > 0, 1.0, 0.0).astype(f32)
    columns_ok = jnp.where(wide < 256, 1.0, jnp.where(wide < 320, north_ok, south_ok))

    def gather(k, carry):
        a = north[k]
        b = south[k]
        for e in range(22):
            ref, x = (before, e) if e < 3 else (field, e - 3) if e < 19 else (after, e - 19)
            ue[k, e, :, 0:256] = ref[k, x]
            right = pltpu.roll(a, 128 - 4 * e, 1) if e else a
            ue[k, e, :, 256:384] = jnp.where(lane < 64, right, pltpu.roll(b, 124 - 4 * e, 1))
        return carry

    lax.fori_loop(0, 9, gather, 0)

    def row_ok(e):
        return jnp.where(e < 3, low_ok, jnp.where(e > 18, high_ok, 1.0))

    def paired(field):
        return 0.5 * (field + jnp.where(even, pltpu.roll(field, 383, 1), pltpu.roll(field, 1, 1)))

    def first(e, carry):
        flux = []
        for node in range(3):
            rows = [[ue[3 * node + c, e + d] for c in range(3)] for d in (-1, 0, 1)]
            flux.append(tendency(*rows, 1, 1.0))
        ok = columns_ok * row_ok(e)
        for c in range(3):
            a, b, d = flux[0][c], flux[1][c], flux[2][c]
            start = ue[c, e]
            new = (start + (one_0 * a + one_1 * b + one_2 * d)) * ok
            v1[c, e] = new
            rest[c, e] = two_0 * a + (two_1 - 0.5 * half_step) * b + two_2 * d
            f0[c, e] = a
            pair_u[c, e] = paired(start)
            pair_v[c, e] = paired(new)
        return carry

    lax.fori_loop(1, 21, first, 0)

    def second(e, carry):
        rows = [[v1[c, e + d] for c in range(3)] for d in (-1, 0, 1)]
        slope = tendency(*rows, 1, 1.0)
        ok = columns_ok * row_ok(e)
        for c in range(3):
            v2[c, e] = (rows[1][c] + (0.5 * half_step) * slope[c] + rest[c, e]) * ok
            h1[c, e] = slope[c]
        return carry

    lax.fori_loop(2, 20, second, 0)

    def moved(e, carry):
        for c in range(3):
            put((native_0, native_1), c * 256, e - 3, v2[c, e])
        return carry

    lax.fori_loop(3, 19, moved, 0)

    for c in range(3):
        for odd in (0, 1):
            for half, native in enumerate((native_0, native_1)):
                one, two = split_pairs(native, c * 256 + odd * 128, turned.at[(c * 2 + odd) * 2 + half])
                halves_2[half * 64:half * 64 + 64, c * 256 + odd * 128:c * 256 + odd * 128 + 128] = 0.5 * (one - two)


def fine_part(place, *arrays):
    vmem = pl.BlockSpec(memory_space=pltpu.VMEM)
    kept = pltpu.VMEM((3, 22, 16, 384), f32)
    return pl.pallas_call(
        fine_body,
        out_shape=[pltpu.VMEM((128, 768), f32)] + [kept] * 6,
        in_specs=[pl.BlockSpec(memory_space=pltpu.SMEM)] + [vmem] * len(arrays),
        out_specs=[vmem] * 7,
        scratch_shapes=[pltpu.VMEM((9, 22, 16, 384), f32), kept]
        + [pltpu.VMEM((768, 128), f32)] * 2
        + [pltpu.VMEM((12, 128, 128), f32)],
        compiler_params=pltpu.CompilerParams(vmem_limit_bytes=36 * 2**20),
        name="fine",
    )(place, *near(*arrays))


def sources_body(place, field, v1, v2, f0, h1, pair_u, pair_v, sources, halves_1, native_0, native_1, turned):
    gy = place[1]
    leader = place[2] == 0
    natives = (native_0, native_1)

    def third(e, carry):
        slope = tendency(*[[v2[c, e + d] for c in range(3)] for d in (-1, 0, 1)], 1, 1.0)
        base_u = tendency(*[[pair_u[c, e + d] for c in range(3)] for d in (-1, 0, 1)], 2, 2.0)
        base_v = tendency(*[[pair_v[c, e + d] for c in range(3)] for d in (-1, 0, 1)], 2, 2.0)
        for c in range(3):
            a, b, d = f0[c, e, :, 0:256], h1[c, e, :, 0:256], slope[c][:, 0:256]
            one = one_0 * a + one_1 * b + one_2 * d
            two = two_0 * a + two_1 * b + two_2 * d
            one = one + jnp.where(leader, field[c, e - 3], (-0.5 * half_step) * base_u[c][:, 0:256])
            two = two - (0.5 * half_step) * base_v[c][:, 0:256]
            put(natives, c * 256, e - 3, one)
            put(natives, (3 + c) * 256, e - 3, two)
            put(natives, (6 + c) * 256, e - 3, v1[c, e, :, 0:256])
        return carry

    lax.fori_loop(3, 19, third, 0)

    def compact(c, carry):
        for part in range(3):
            for odd in (0, 1):
                start = pl.multiple_of((part * 3 + c) * 256 + odd * 128, 128)
                for half, native in enumerate(natives):
                    one, two = split_pairs(native, start, turned.at[(part * 2 + odd) * 2 + half])
                    tile = pl.multiple_of(c * 256 + odd * 128, 128)
                    if part == 2:
                        halves_1[pl.ds(half * 64, 64), pl.ds(tile, 128)] = 0.5 * (one - two)
                    else:
                        mean = 0.5 * (one + two)
                        for i in range(8):
                            to = device_of(half * 8 + i, gy)
                            sources[to, :, pl.ds(part * 768 + tile, 128)] = mean[8 * i:8 * i + 8]
        return carry

    lax.fori_loop(0, 3, compact, 0)


def sources_part(place, *arrays):
    vmem = pl.BlockSpec(memory_space=pltpu.VMEM)
    return pl.pallas_call(
        sources_body,
        out_shape=(pltpu.VMEM((16, 8, 1536), f32), jax.ShapeDtypeStruct((128, 768), f32)),
        in_specs=[pl.BlockSpec(memory_space=pltpu.SMEM)] + [vmem] * len(arrays),
        out_specs=[vmem] * 2,
        scratch_shapes=[pltpu.VMEM((2304, 128), f32)] * 2 + [pltpu.VMEM((12, 128, 128), f32)],
        compiler_params=pltpu.CompilerParams(vmem_limit_bytes=16 * 2**20),
        name="sources",
    )(place, *near(*arrays))


def pack_body(source, to_right, to_left):
    row = lax.broadcasted_iota(jnp.int32, (8, 768), 0)
    for j in range(2):
        for field in range(2):
            k = 2 * j + field
            for xh in range(4):
                one = source[j * 4 + xh, :, field * 768:(field + 1) * 768]
                two = source[(3 - j) * 4 + xh, :, (1 - field) * 768:(2 - field) * 768]
                right = pltpu.roll(two, k, 0) if k else two
                left = pltpu.roll(two, 8 - k, 0) if k else two
                to_right[j * 4 + xh, :, field * 768:(field + 1) * 768] = jnp.where(row > k, one, right)
                to_left[j * 4 + xh, :, field * 768:(field + 1) * 768] = jnp.where(row < 7 - k, one, left)


def pack(source):
    vmem = pl.BlockSpec(memory_space=pltpu.VMEM)
    shape = pltpu.VMEM((8, 8, 1536), f32)
    return pl.pallas_call(
        pack_body,
        in_specs=[vmem],
        out_specs=[vmem] * 2,
        out_shape=(shape, shape),
        compiler_params=pltpu.CompilerParams(vmem_limit_bytes=8 * 2**20),
        name="pack",
    )(*near(source))


def stage_body(place, *rest, begins, ends):
    rest = list(rest)
    starts = () if begins else (rest.pop(0), rest.pop(0), rest.pop(0))
    source, source_left, source_right, result, buffer_0, buffer_1 = rest
    lane = lanes((24, 128))
    x_first = lane % 8 == 0
    x_last = lane % 8 == 7
    row = lax.broadcasted_iota(jnp.int32, (24, 128), 0)
    inside = ((row >= 8) | (place[3] > 0)) & ((row < 16) | (place[3] < 63))

    for c in range(3):
        for t in range(8):
            for buffer in (buffer_0, buffer_1):
                buffer[c, t, 0:8] = jnp.zeros((8, 128), f32)
                buffer[c, t, 32:40] = jnp.zeros((8, 128), f32)
            if begins:
                buffer_0[c, t, 8:32] = jnp.zeros((24, 128), f32)
            else:
                own, left, right = starts
                buffer_0[c, t, 8:16] = left[c, t]
                buffer_0[c, t, 16:24] = own[c, t]
                buffer_0[c, t, 24:32] = right[c, t]

    def keep(j, field, buffer):
        for xh in range(4):
            for c in range(3):
                for odd in range(2):
                    at = (field * 6 + c * 2 + odd) * 128
                    result[j * 4 + xh, :, at:at + 128] = buffer[c, xh * 2 + odd, 16:24]

    square = 0.25
    c_side = half_step * viscosity
    c_second = half_step * viscosity * square
    c_centre = 1.0 - half_step * viscosity * (4.0 + 2.0 * square)

    def step(j, field, old, new, late):
        k = 2 * j + field
        for xh in range(4):
            for odd in range(2):
                t = 2 * xh + odd
                u = [old[c, t, 8:32] for c in range(3)]
                k0 = u[0] * (-0.5 * half_step)
                k1 = u[1] * (-0.25 * half_step)
                k2 = u[2] * (-0.5 * half_step)
                for c in range(3):
                    v = u[c]
                    other = old[c, t + 1 - 2 * odd, 8:32]
                    if odd:
                        beyond = pltpu.roll(old[c, t + 1, 8:32], 7, 1) if xh < 3 else 0.0
                        east = jnp.where(x_last, beyond, pltpu.roll(other, 127, 1))
                        west = other
                    else:
                        beyond = pltpu.roll(old[c, t - 1, 8:32], 121, 1) if xh > 0 else 0.0
                        east = other
                        west = jnp.where(x_first, beyond, pltpu.roll(other, 1, 1))
                    up = pltpu.roll(v, 120, 1)
                    down = pltpu.roll(v, 8, 1)
                    north = old[c, t, 9:33]
                    south = old[c, t, 7:31]
                    at = (field * 6 + c * 2 + odd) * 128
                    if late:
                        there = ((1 - field) * 6 + c * 2 + odd) * 128
                        pull_left = pltpu.roll(source_left[(3 - j) * 4 + xh, :, there:there + 128], (1 + k) % 8, 0)
                        pull_right = pltpu.roll(source_right[(3 - j) * 4 + xh, :, there:there + 128], 7 - k, 0)
                    else:
                        pull_left = source_left[j * 4 + xh, :, at:at + 128]
                        pull_right = source_right[j * 4 + xh, :, at:at + 128]
                    pull = jnp.concatenate(
                        [pull_left, source[j * 4 + xh, :, at:at + 128], pull_right], axis=0
                    )
                    value = (
                        c_centre * v
                        + c_side * ((east + west) + (up + down))
                        + c_second * (north + south)
                        + (k0 * (east - west) + k1 * (north - south) + k2 * (up - down))
                        + pull
                    )
                    new[c, t, 8:32] = jnp.where(inside, value, 0.0)

    def one_slice(j, late):
        if ends:
            keep(j, 0, buffer_0)
        step(j, 0, buffer_0, buffer_1, late)
        if ends:
            keep(j, 1, buffer_1)
        step(j, 1, buffer_1, buffer_0, late)
        if ends:
            keep(j, 2, buffer_0)

    def early(j, carry):
        one_slice(j, False)
        return carry

    def later(j, carry):
        one_slice(j, True)
        return carry

    lax.fori_loop(0, 2, early, 0)
    lax.fori_loop(2, 4, later, 0)
    if not ends:
        for c in range(3):
            for t in range(8):
                result[c, t] = buffer_0[c, t, 16:24]


def stage(place, starts, sources, ends):
    vmem = pl.BlockSpec(memory_space=pltpu.VMEM)
    arrays = near(*starts, *sources)
    return pl.pallas_call(
        functools.partial(stage_body, begins=not starts, ends=ends),
        out_shape=pltpu.VMEM((16, 8, 2304) if ends else (3, 8, 8, 128), f32),
        in_specs=[pl.BlockSpec(memory_space=pltpu.SMEM)] + [vmem] * len(arrays),
        out_specs=vmem,
        scratch_shapes=[pltpu.VMEM((3, 8, 40, 128), f32)] * 2,
        compiler_params=pltpu.CompilerParams(vmem_limit_bytes=12 * 2**20),
        name="stage",
    )(place, *arrays)


def finish_body(place, start, coarse, halves_0, halves_1, halves_2, out, mixed, rows):
    gy = place[1]

    def one_field(field, halves):
        for c in range(3):
            for half in range(2):
                for odd in range(2):
                    tile = pl.ds(field * 768 + c * 256 + odd * 128, 128)
                    w = jnp.concatenate(
                        [coarse[device_of(half * 8 + i, gy), :, tile] for i in range(8)], axis=0
                    )
                    e = halves[pl.ds(half * 64, 64), pl.ds(c * 256 + odd * 128, 128)]
                    at = (c * 2 + half) * 2 + odd
                    mixed[at, pl.ds(0, 64, stride=2), :] = w + e
                    mixed[at, pl.ds(1, 64, stride=2), :] = w - e
                    rows[c * 2 + half, pl.ds(odd, 128, stride=2), :] = mixed[at].T
                out[pl.ds(c * 32, 32), half] = rows[c * 2 + half].reshape(32, 8, 128)

    for field, halves in enumerate((halves_0, halves_1, halves_2)):
        if field:
            chosen = pl.program_id(0) == field
        else:
            chosen = (pl.program_id(0) == 0) & (place[2] > 0)
        pl.when(chosen)(functools.partial(one_field, field, halves))

    @pl.when((pl.program_id(0) == 0) & (place[2] == 0))
    def _():
        pltpu.sync_copy(start.at[pl.ds(0, 96)], out)


def finish(place, start, coarse, *halves):
    vmem = pl.BlockSpec(memory_space=pltpu.VMEM)
    return pl.pallas_call(
        finish_body,
        grid=(3,),
        out_shape=jax.ShapeDtypeStruct((288, 2, 8, 128), f32),
        in_specs=[pl.BlockSpec(memory_space=pltpu.SMEM), pl.BlockSpec(memory_space=pl.ANY)] + [vmem] * 4,
        out_specs=pl.BlockSpec((96, 2, 8, 128), lambda f: (f, 0, 0, 0)),
        scratch_shapes=[pltpu.VMEM((12, 128, 128), f32), pltpu.VMEM((6, 256, 128), f32)],
        compiler_params=pltpu.CompilerParams(vmem_limit_bytes=16 * 2**20),
        name="finish",
    )(place, start, *near(coarse), *halves)


def sent(block, axes, sizes, moves):
    strides = {}
    total = 1
    for axis in reversed(axes):
        strides[axis] = total
        total *= sizes[axis]
    pairs = []
    for source in range(total):
        target = source
        for axis, by in moves.items():
            at = source // strides[axis] % sizes[axis]
            if not 0 <= at + by < sizes[axis]:
                target = None
                break
            target += by * strides[axis]
        if target is not None:
            pairs.append((source, target))
    return lax.ppermute(block, axes if len(axes) > 1 else axes[0], pairs)


def solution(mesh):
    sizes = {"tz": 4, "ty": 4, "gx": 4, "gy": 4}
    fine_mesh = Mesh(mesh.devices.reshape(4, 4, 4, 4), tuple(sizes))
    pieces = ("ty", "gx", "gy")

    def beside(block, by):
        def name(piece):
            gy, at = divmod(piece, 16)
            return snake(15 - at if gy % 2 else at) * 4 + gy

        pairs = [(name(i), name(i + by)) for i in range(64) if 0 <= i + by < 64]
        return lax.ppermute(block, pieces, pairs)

    def per_device(provisional):
        tz, ty, gx, gy = (lax.axis_index(a) for a in sizes)
        piece = ty * 4 + jnp.where(ty % 2 == 0, gx, 3 - gx)
        piece = gy * 16 + jnp.where(gy % 2 == 0, piece, 15 - piece)
        place = jnp.stack([gx, gy, tz * 4 + ty, piece]).astype(jnp.int32)
        tiles = provisional.reshape(288, 8, 2, 128).transpose(0, 2, 1, 3)
        held, low_rows, high_rows = edges(tiles.reshape(4608, 128))
        after = sent(low_rows, ("gx",), sizes, {"gx": -1})
        before = sent(high_rows, ("gx",), sizes, {"gx": 1})
        field = turned_field(held)
        low_columns, high_columns = columns(field, before, after)
        south = sent(high_columns, ("gy",), sizes, {"gy": 1})
        north = sent(low_columns, ("gy",), sizes, {"gy": -1})
        halves_2, *kept = fine_part(place, field, before, after, south, north)
        halves_0 = lax.ppermute(halves_2, ("tz", "ty"), [(i, i + 1) for i in range(15)])
        sources, halves_1 = sources_part(place, field, *kept)
        source = lax.all_to_all(sources, group_axes, 0, 0)
        to_right, to_left = pack(source)
        source_left = beside(to_right, 1)
        source_right = beside(to_left, -1)
        starts = ()
        for turn in range(4):
            own = stage(place, starts, (source, source_left, source_right), turn == 3)
            if turn < 3:
                own = sent(own, ("tz",), sizes, {"tz": 1})
                starts = (own, beside(own, 1), beside(own, -1))
            if turn == 2:
                starts, halves_0 = lax.optimization_barrier((starts, halves_0))
        coarse = lax.all_to_all(own, group_axes, 0, 0)
        out = finish(place, tiles, coarse, halves_0, halves_1, halves_2)
        return out.transpose(0, 2, 1, 3).reshape(1, 3, 3, 16, 16, 256)

    spec = P(("tz", "ty"), None, None, None, "gx", "gy")

    return jax.shard_map(per_device, mesh=fine_mesh, in_specs=(spec,), out_specs=spec, check_vma=False)
```

```python
import functools

import jax
import jax.numpy as jnp
from jax import lax
from jax.experimental import pallas as pl
from jax.experimental.pallas import tpu as pltpu
from jax.sharding import Mesh
from jax.sharding import PartitionSpec as P


viscosity = 0.1
slice_step = 0.25
half_step = 0.125
first_row = (5.0 / 24.0, 1.0 / 3.0, -1.0 / 24.0)
second_row = (-1.0 / 24.0, 1.0 / 3.0, 5.0 / 24.0)

f32 = jnp.float32
group_axes = ("ty", "gx")


def snake(piece):
    return piece if piece // 4 % 2 == 0 else piece // 4 * 4 + 3 - piece % 4


def device_of(piece, gy):
    return jnp.where(gy % 2 == 0, snake(piece), snake(15 - piece))


def near(*arrays):
    return tuple(pltpu.with_memory_space_constraint(a, pltpu.VMEM) for a in arrays)


def lanes(shape):
    return lax.broadcasted_iota(jnp.int32, shape, len(shape) - 1)


def strided(u, k, x, half):
    at = k * 512 + x // 8 * 16 + half * 8 + x % 8
    return jnp.concatenate([u[pl.ds(at + 32 * odd, 8, stride=64), :] for odd in (0, 1)], axis=0)


def edges_body(u, held, low_rows, high_rows, arrived):
    copies = [
        pltpu.make_async_copy(u.at[pl.ds(512 * k, 512)], held.at[pl.ds(512 * k, 512)], arrived.at[k])
        for k in range(9)
    ]
    for copy in copies:
        copy.start()
    for k in range(9):
        copies[k].wait()
        for x in (0, 1, 2, 13, 14, 15):
            to = low_rows.at[k, x] if x < 3 else high_rows.at[k, x - 13]
            for half in range(2):
                to[:, half * 128:(half + 1) * 128] = strided(held, k, x, half)


def edges(u):
    vmem = pl.BlockSpec(memory_space=pltpu.VMEM)
    rows = pltpu.VMEM((9, 3, 16, 256), f32)
    return pl.pallas_call(
        edges_body,
        in_specs=[pl.BlockSpec(memory_space=pltpu.HBM)],
        out_specs=[vmem] * 3,
        out_shape=(pltpu.VMEM((4608, 128), f32), rows, rows),
        scratch_shapes=[pltpu.SemaphoreType.DMA((9,))],
        compiler_params=pltpu.CompilerParams(vmem_limit_bytes=12 * 2**20),
        name="edges",
    )(pltpu.with_memory_space_constraint(u, pltpu.HBM))


def turned_body(held, field):
    def each(k, carry):
        for x in range(16):
            for half in range(2):
                field[k, x, :, half * 128:(half + 1) * 128] = strided(held, k, x, half)
        return carry

    lax.fori_loop(0, 9, each, 0)


def turned_field(held):
    vmem = pl.BlockSpec(memory_space=pltpu.VMEM)
    return pl.pallas_call(
        turned_body,
        in_specs=[vmem],
        out_specs=vmem,
        out_shape=pltpu.VMEM((9, 16, 16, 256), f32),
        compiler_params=pltpu.CompilerParams(vmem_limit_bytes=8 * 2**20),
        name="turned",
    )(*near(held))


def columns_body(field, before, after, low, high):
    lane = lanes((16, 128))

    def each(k, carry):
        for t in range(3):
            one = jnp.zeros((16, 128), f32)
            two = jnp.zeros((16, 128), f32)
            for e in range(8 * t, min(8 * t + 8, 22)):
                ref, x = (before, e) if e < 3 else (field, e - 3) if e < 19 else (after, e - 19)
                at = e % 8 * 16
                turned_one = pltpu.roll(ref[k, x, :, 0:128], at + 4, 1)
                turned_two = pltpu.roll(ref[k, x, :, 128:256], (at + 12) % 128, 1)
                one = jnp.where((lane >= at + 4) & (lane < at + 16), turned_one, one)
                two = jnp.where((lane >= at) & (lane < at + 12), turned_two, two)
            low[k, :, t * 128:(t + 1) * 128] = one
            high[k, :, t * 128:(t + 1) * 128] = two
        return carry

    lax.fori_loop(0, 9, each, 0)


def columns(field, before, after):
    vmem = pl.BlockSpec(memory_space=pltpu.VMEM)
    shape = pltpu.VMEM((9, 16, 384), f32)
    return pl.pallas_call(
        columns_body,
        in_specs=[vmem] * 3,
        out_specs=[vmem] * 2,
        out_shape=(shape, shape),
        compiler_params=pltpu.CompilerParams(vmem_limit_bytes=8 * 2**20),
        name="columns",
    )(*near(field, before, after))


def tendency(below, row, above, reach, spacing):
    width = row[0].shape[-1]
    square = 1.0 / (spacing * spacing)
    out = []
    for c in range(3):
        u = row[c]
        up = jnp.concatenate([u[8:16], pltpu.roll(u[0:8], 7, 0)], axis=0)
        down = jnp.concatenate([pltpu.roll(u[8:16], 1, 0), u[0:8]], axis=0)
        north = pltpu.roll(u, width - reach, 1)
        south = pltpu.roll(u, reach, 1)
        laplace = (above[c] + below[c]) + (up + down) - (4.0 + 2.0 * square) * u
        laplace = laplace + (north + south) * square
        transport = (
            row[0] * (above[c] - below[c])
            + row[1] * ((north - south) * (1.0 / spacing))
            + row[2] * (up - down)
        )
        out.append((2.0 * viscosity) * laplace - transport)
    return out


quarter = 0.5 * slice_step
one_0, one_1, one_2 = (quarter * w for w in first_row)
two_0, two_1, two_2 = (quarter * w for w in second_row)


def put(natives, base, x, value):
    for odd in (0, 1):
        at = pl.ds(base + x % 2 * 128 + x // 2 + odd * 8, 8, stride=16)
        for half, native in enumerate(natives):
            native[at, :] = value[odd * 8:odd * 8 + 8, half * 128:(half + 1) * 128]


def split_pairs(native, start, scratch):
    scratch[...] = native[pl.ds(start, 128), :].T
    return scratch[pl.ds(0, 64, stride=2), :], scratch[pl.ds(1, 64, stride=2), :]


def edge_factor(place, axis, low):
    return jnp.where(place[axis] > 0 if low else place[axis] < 3, 1.0, 0.0).astype(f32)


def paired(field):
    width = field.shape[-1]
    even = lanes(field.shape) % 2 == 0
    return 0.5 * (field + jnp.where(even, pltpu.roll(field, width - 1, 1), pltpu.roll(field, 1, 1)))


def swept(rows_of):
    flux = [tendency(*rows_of(node), 1, 1.0) for node in range(3)]
    start = rows_of(0)[1]
    new = [start[c] + (one_0 * flux[0][c] + one_1 * flux[1][c] + one_2 * flux[2][c]) for c in range(3)]
    rest = [two_0 * flux[0][c] + (two_1 - 0.5 * half_step) * flux[1][c] + two_2 * flux[2][c] for c in range(3)]
    return new, rest, flux[0]


def source_pair(leader, start, a, b, d, base_u, base_v):
    one = one_0 * a + one_1 * b + one_2 * d
    two = two_0 * a + two_1 * b + two_2 * d
    one = one + jnp.where(leader, start, (-0.5 * half_step) * base_u)
    return one, two - (0.5 * half_step) * base_v


def fine_body(place, field, before, after, v1, v2, f0, h1, pair_u, pair_v, ue, rest):
    low_ok = edge_factor(place, 0, True)
    high_ok = edge_factor(place, 0, False)

    def gather(k, carry):
        for e in range(22):
            ref, x = (before, e) if e < 3 else (field, e - 3) if e < 19 else (after, e - 19)
            ue[k, e] = ref[k, x]
        return carry

    lax.fori_loop(0, 9, gather, 0)

    def row_ok(e):
        return jnp.where(e < 3, low_ok, jnp.where(e > 18, high_ok, 1.0))

    def first(e, carry):
        new, more, flux = swept(lambda node: [[ue[3 * node + c, e + d] for c in range(3)] for d in (-1, 0, 1)])
        for c in range(3):
            value = new[c] * row_ok(e)
            v1[c, e] = value
            rest[c, e] = more[c]
            f0[c, e] = flux[c]
            pair_u[c, e] = paired(ue[c, e])
            pair_v[c, e] = paired(value)
        return carry

    lax.fori_loop(1, 21, first, 0)

    def second(e, carry):
        rows = [[v1[c, e + d] for c in range(3)] for d in (-1, 0, 1)]
        slope = tendency(*rows, 1, 1.0)
        for c in range(3):
            v2[c, e] = (rows[1][c] + (0.5 * half_step) * slope[c] + rest[c, e]) * row_ok(e)
            h1[c, e] = slope[c]
        return carry

    lax.fori_loop(2, 20, second, 0)


def fine_part(place, *arrays):
    vmem = pl.BlockSpec(memory_space=pltpu.VMEM)
    kept = pltpu.VMEM((3, 22, 16, 256), f32)
    return pl.pallas_call(
        fine_body,
        out_shape=[kept] * 6,
        in_specs=[pl.BlockSpec(memory_space=pltpu.SMEM)] + [vmem] * len(arrays),
        out_specs=[vmem] * 6,
        scratch_shapes=[pltpu.VMEM((9, 22, 16, 256), f32), kept],
        compiler_params=pltpu.CompilerParams(vmem_limit_bytes=28 * 2**20),
        name="fine",
    )(place, *near(*arrays))


def strip_body(place, low, high, south, north, strips):
    lane = lanes((16, 768))
    row = lane % 384 // 16
    south_side = (lane < 384) & (lane % 16 < 4)
    north_side = (lane >= 384) & (lane % 16 > 11)
    column_ok = jnp.where(south_side, edge_factor(place, 1, True), jnp.where(north_side, edge_factor(place, 1, False), 1.0))
    rows_ok = jnp.where(row < 3, edge_factor(place, 0, True), jnp.where(row > 18, edge_factor(place, 0, False), 1.0))
    ok = column_ok * rows_ok
    slot = lanes((16, 384)) % 16

    def whole(k):
        left = jnp.where(slot < 4, pltpu.roll(south[k], 376, 1), low[k])
        right = jnp.where(slot > 11, pltpu.roll(north[k], 8, 1), high[k])
        return jnp.concatenate([left, right], axis=1)

    def around(rows):
        return [pltpu.roll(r, 16, 1) for r in rows], rows, [pltpu.roll(r, 752, 1) for r in rows]

    u = [[whole(3 * node + c) for c in range(3)] for node in range(3)]
    nodes = [around(u[node]) for node in range(3)]
    new, more, flux = swept(lambda node: nodes[node])
    v1 = [value * ok for value in new]
    h1 = tendency(*around(v1), 1, 1.0)
    v2 = [(v1[c] + (0.5 * half_step) * h1[c] + more[c]) * ok for c in range(3)]
    h2 = tendency(*around(v2), 1, 1.0)
    base_u = tendency(*around([paired(x) for x in u[0]]), 2, 2.0)
    base_v = tendency(*around([paired(x) for x in v1]), 2, 2.0)
    for c in range(3):
        one, two = source_pair(place[2] == 0, u[0][c], flux[c], h1[c], h2[c], base_u[c], base_v[c])
        for part, value in enumerate((one, two, v1[c], v2[c])):
            for t in range(6):
                strips[part * 3 + c, t] = value[:, t * 128:(t + 1) * 128]


def strip_part(place, *arrays):
    vmem = pl.BlockSpec(memory_space=pltpu.VMEM)
    return pl.pallas_call(
        strip_body,
        out_shape=pltpu.VMEM((12, 6, 16, 128), f32),
        in_specs=[pl.BlockSpec(memory_space=pltpu.SMEM)] + [vmem] * 4,
        out_specs=vmem,
        compiler_params=pltpu.CompilerParams(vmem_limit_bytes=8 * 2**20),
        name="strip",
    )(place, *near(*arrays))


def joined(value, strips, at, e):
    lane = lanes((16, 128))
    shift = e % 8 * 16
    left = pltpu.roll(strips[at, e // 8], 124 - shift, 1)
    right = pltpu.roll(strips[at, 3 + e // 8], 116 - shift, 1)
    low = jnp.where(lane < 4, left, value[:, 0:128])
    high = jnp.where(lane >= 124, right, value[:, 128:256])
    return jnp.concatenate([low, high], axis=1)


def halves_body(values, strips, halves, native_0, native_1, turned, part):
    def moved(e, carry):
        for c in range(3):
            put((native_0, native_1), c * 256, e - 3, joined(values[c, e], strips, part * 3 + c, e))
        return carry

    lax.fori_loop(3, 19, moved, 0)

    for c in range(3):
        for odd in (0, 1):
            tile = c * 256 + odd * 128
            for half, native in enumerate((native_0, native_1)):
                one, two = split_pairs(native, tile, turned.at[(c * 2 + odd) * 2 + half])
                halves[half * 64:half * 64 + 64, tile:tile + 128] = 0.5 * (one - two)


def halves_part(values, strips, part):
    vmem = pl.BlockSpec(memory_space=pltpu.VMEM)
    return pl.pallas_call(
        functools.partial(halves_body, part=part),
        out_shape=pltpu.VMEM((128, 768), f32),
        in_specs=[vmem] * 2,
        out_specs=vmem,
        scratch_shapes=[pltpu.VMEM((768, 128), f32)] * 2 + [pltpu.VMEM((12, 128, 128), f32)],
        compiler_params=pltpu.CompilerParams(vmem_limit_bytes=8 * 2**20),
        name="halves",
    )(*near(values, strips))


def sources_body(place, field, strips, v2, f0, h1, pair_u, pair_v, sources, native_0, native_1, turned):
    gy = place[1]
    leader = place[2] == 0
    natives = (native_0, native_1)

    def third(e, carry):
        slope = tendency(*[[v2[c, e + d] for c in range(3)] for d in (-1, 0, 1)], 1, 1.0)
        base_u = tendency(*[[pair_u[c, e + d] for c in range(3)] for d in (-1, 0, 1)], 2, 2.0)
        base_v = tendency(*[[pair_v[c, e + d] for c in range(3)] for d in (-1, 0, 1)], 2, 2.0)
        for c in range(3):
            both = source_pair(leader, field[c, e - 3], f0[c, e], h1[c, e], slope[c], base_u[c], base_v[c])
            for part, value in enumerate(both):
                put(natives, (3 * part + c) * 256, e - 3, joined(value, strips, 3 * part + c, e))
        return carry

    lax.fori_loop(3, 19, third, 0)

    def compact(c, carry):
        for part in range(2):
            for odd in (0, 1):
                start = pl.multiple_of((part * 3 + c) * 256 + odd * 128, 128)
                for half, native in enumerate(natives):
                    one, two = split_pairs(native, start, turned.at[(part * 2 + odd) * 2 + half])
                    mean = 0.5 * (one + two)
                    tile = pl.multiple_of(part * 768 + c * 256 + odd * 128, 128)
                    for i in range(8):
                        sources[device_of(half * 8 + i, gy), :, pl.ds(tile, 128)] = mean[8 * i:8 * i + 8]
        return carry

    lax.fori_loop(0, 3, compact, 0)


def sources_part(place, *arrays):
    vmem = pl.BlockSpec(memory_space=pltpu.VMEM)
    return pl.pallas_call(
        sources_body,
        out_shape=pltpu.VMEM((16, 8, 1536), f32),
        in_specs=[pl.BlockSpec(memory_space=pltpu.SMEM)] + [vmem] * len(arrays),
        out_specs=vmem,
        scratch_shapes=[pltpu.VMEM((1536, 128), f32)] * 2 + [pltpu.VMEM((8, 128, 128), f32)],
        compiler_params=pltpu.CompilerParams(vmem_limit_bytes=16 * 2**20),
        name="sources",
    )(place, *near(*arrays))


def pack_body(source, to_right, to_left):
    row = lax.broadcasted_iota(jnp.int32, (8, 768), 0)
    for j in range(2):
        for field in range(2):
            k = 2 * j + field
            for xh in range(4):
                one = source[j * 4 + xh, :, field * 768:(field + 1) * 768]
                two = source[(3 - j) * 4 + xh, :, (1 - field) * 768:(2 - field) * 768]
                right = pltpu.roll(two, k, 0) if k else two
                left = pltpu.roll(two, 8 - k, 0) if k else two
                to_right[j * 4 + xh, :, field * 768:(field + 1) * 768] = jnp.where(row > k, one, right)
                to_left[j * 4 + xh, :, field * 768:(field + 1) * 768] = jnp.where(row < 7 - k, one, left)


def pack(source):
    vmem = pl.BlockSpec(memory_space=pltpu.VMEM)
    shape = pltpu.VMEM((8, 8, 1536), f32)
    return pl.pallas_call(
        pack_body,
        in_specs=[vmem],
        out_specs=[vmem] * 2,
        out_shape=(shape, shape),
        compiler_params=pltpu.CompilerParams(vmem_limit_bytes=8 * 2**20),
        name="pack",
    )(*near(source))


def stage_body(place, *rest, begins, ends):
    rest = list(rest)
    starts = () if begins else (rest.pop(0), rest.pop(0), rest.pop(0))
    source, source_left, source_right, result, buffer_0, buffer_1 = rest
    lane = lanes((24, 128))
    x_first = lane % 8 == 0
    x_last = lane % 8 == 7
    row = lax.broadcasted_iota(jnp.int32, (24, 128), 0)
    inside = ((row >= 8) | (place[3] > 0)) & ((row < 16) | (place[3] < 63))

    for c in range(3):
        for t in range(8):
            for buffer in (buffer_0, buffer_1):
                buffer[c, t, 0:8] = jnp.zeros((8, 128), f32)
                buffer[c, t, 32:40] = jnp.zeros((8, 128), f32)
            if begins:
                buffer_0[c, t, 8:32] = jnp.zeros((24, 128), f32)
            else:
                own, left, right = starts
                buffer_0[c, t, 8:16] = left[c, t]
                buffer_0[c, t, 16:24] = own[c, t]
                buffer_0[c, t, 24:32] = right[c, t]

    def keep(j, field, buffer):
        for xh in range(4):
            for c in range(3):
                for odd in range(2):
                    at = (field * 6 + c * 2 + odd) * 128
                    result[j * 4 + xh, :, at:at + 128] = buffer[c, xh * 2 + odd, 16:24]

    square = 0.25
    c_side = half_step * viscosity
    c_second = half_step * viscosity * square
    c_centre = 1.0 - half_step * viscosity * (4.0 + 2.0 * square)

    def step(j, field, old, new, late):
        k = 2 * j + field
        for xh in range(4):
            for odd in range(2):
                t = 2 * xh + odd
                u = [old[c, t, 8:32] for c in range(3)]
                k0 = u[0] * (-0.5 * half_step)
                k1 = u[1] * (-0.25 * half_step)
                k2 = u[2] * (-0.5 * half_step)
                for c in range(3):
                    v = u[c]
                    other = old[c, t + 1 - 2 * odd, 8:32]
                    if odd:
                        beyond = pltpu.roll(old[c, t + 1, 8:32], 7, 1) if xh < 3 else 0.0
                        east = jnp.where(x_last, beyond, pltpu.roll(other, 127, 1))
                        west = other
                    else:
                        beyond = pltpu.roll(old[c, t - 1, 8:32], 121, 1) if xh > 0 else 0.0
                        east = other
                        west = jnp.where(x_first, beyond, pltpu.roll(other, 1, 1))
                    up = pltpu.roll(v, 120, 1)
                    down = pltpu.roll(v, 8, 1)
                    north = old[c, t, 9:33]
                    south = old[c, t, 7:31]
                    at = (field * 6 + c * 2 + odd) * 128
                    if late:
                        there = ((1 - field) * 6 + c * 2 + odd) * 128
                        pull_left = pltpu.roll(source_left[(3 - j) * 4 + xh, :, there:there + 128], (1 + k) % 8, 0)
                        pull_right = pltpu.roll(source_right[(3 - j) * 4 + xh, :, there:there + 128], 7 - k, 0)
                    else:
                        pull_left = source_left[j * 4 + xh, :, at:at + 128]
                        pull_right = source_right[j * 4 + xh, :, at:at + 128]
                    pull = jnp.concatenate(
                        [pull_left, source[j * 4 + xh, :, at:at + 128], pull_right], axis=0
                    )
                    value = (
                        c_centre * v
                        + c_side * ((east + west) + (up + down))
                        + c_second * (north + south)
                        + (k0 * (east - west) + k1 * (north - south) + k2 * (up - down))
                        + pull
                    )
                    new[c, t, 8:32] = jnp.where(inside, value, 0.0)

    def one_slice(j, late):
        if ends:
            keep(j, 0, buffer_0)
        step(j, 0, buffer_0, buffer_1, late)
        if ends:
            keep(j, 1, buffer_1)
        step(j, 1, buffer_1, buffer_0, late)
        if ends:
            keep(j, 2, buffer_0)

    def early(j, carry):
        one_slice(j, False)
        return carry

    def later(j, carry):
        one_slice(j, True)
        return carry

    lax.fori_loop(0, 2, early, 0)
    lax.fori_loop(2, 4, later, 0)
    if not ends:
        for c in range(3):
            for t in range(8):
                result[c, t] = buffer_0[c, t, 16:24]


def stage(place, starts, sources, ends):
    vmem = pl.BlockSpec(memory_space=pltpu.VMEM)
    arrays = near(*starts, *sources)
    return pl.pallas_call(
        functools.partial(stage_body, begins=not starts, ends=ends),
        out_shape=pltpu.VMEM((16, 8, 2304) if ends else (3, 8, 8, 128), f32),
        in_specs=[pl.BlockSpec(memory_space=pltpu.SMEM)] + [vmem] * len(arrays),
        out_specs=vmem,
        scratch_shapes=[pltpu.VMEM((3, 8, 40, 128), f32)] * 2,
        compiler_params=pltpu.CompilerParams(vmem_limit_bytes=12 * 2**20),
        name="stage",
    )(place, *arrays)


def finish_body(place, start, coarse, halves_0, halves_1, halves_2, out, mixed, rows):
    gy = place[1]

    def one_field(field, halves):
        for c in range(3):
            for half in range(2):
                for odd in range(2):
                    tile = pl.ds(field * 768 + c * 256 + odd * 128, 128)
                    w = jnp.concatenate(
                        [coarse[device_of(half * 8 + i, gy), :, tile] for i in range(8)], axis=0
                    )
                    e = halves[pl.ds(half * 64, 64), pl.ds(c * 256 + odd * 128, 128)]
                    at = (c * 2 + half) * 2 + odd
                    mixed[at, pl.ds(0, 64, stride=2), :] = w + e
                    mixed[at, pl.ds(1, 64, stride=2), :] = w - e
                    rows[c * 2 + half, pl.ds(odd, 128, stride=2), :] = mixed[at].T
                out[pl.ds(c * 32, 32), half] = rows[c * 2 + half].reshape(32, 8, 128)

    for field, halves in enumerate((halves_0, halves_1, halves_2)):
        if field:
            chosen = pl.program_id(0) == field
        else:
            chosen = (pl.program_id(0) == 0) & (place[2] > 0)
        pl.when(chosen)(functools.partial(one_field, field, halves))

    @pl.when((pl.program_id(0) == 0) & (place[2] == 0))
    def _():
        pltpu.sync_copy(start.at[pl.ds(0, 96)], out)


def finish(place, start, coarse, *halves):
    vmem = pl.BlockSpec(memory_space=pltpu.VMEM)
    return pl.pallas_call(
        finish_body,
        grid=(3,),
        out_shape=jax.ShapeDtypeStruct((288, 2, 8, 128), f32),
        in_specs=[pl.BlockSpec(memory_space=pltpu.SMEM), pl.BlockSpec(memory_space=pl.ANY)] + [vmem] * 4,
        out_specs=pl.BlockSpec((96, 2, 8, 128), lambda f: (f, 0, 0, 0)),
        scratch_shapes=[pltpu.VMEM((12, 128, 128), f32), pltpu.VMEM((6, 256, 128), f32)],
        compiler_params=pltpu.CompilerParams(vmem_limit_bytes=16 * 2**20),
        name="finish",
    )(place, start, *near(coarse), *halves)


def sent(block, axes, sizes, moves):
    strides = {}
    total = 1
    for axis in reversed(axes):
        strides[axis] = total
        total *= sizes[axis]
    pairs = []
    for source in range(total):
        target = source
        for axis, by in moves.items():
            at = source // strides[axis] % sizes[axis]
            if not 0 <= at + by < sizes[axis]:
                target = None
                break
            target += by * strides[axis]
        if target is not None:
            pairs.append((source, target))
    return lax.ppermute(block, axes if len(axes) > 1 else axes[0], pairs)


def solution(mesh):
    sizes = {"tz": 4, "ty": 4, "gx": 4, "gy": 4}
    fine_mesh = Mesh(mesh.devices.reshape(4, 4, 4, 4), tuple(sizes))
    pieces = ("ty", "gx", "gy")

    def beside(block, by):
        def name(piece):
            gy, at = divmod(piece, 16)
            return snake(15 - at if gy % 2 else at) * 4 + gy

        pairs = [(name(i), name(i + by)) for i in range(64) if 0 <= i + by < 64]
        return lax.ppermute(block, pieces, pairs)

    def per_device(provisional):
        tz, ty, gx, gy = (lax.axis_index(a) for a in sizes)
        piece = ty * 4 + jnp.where(ty % 2 == 0, gx, 3 - gx)
        piece = gy * 16 + jnp.where(gy % 2 == 0, piece, 15 - piece)
        place = jnp.stack([gx, gy, tz * 4 + ty, piece]).astype(jnp.int32)
        tiles = provisional.reshape(288, 8, 2, 128).transpose(0, 2, 1, 3)
        held, low_rows, high_rows = edges(tiles.reshape(4608, 128))
        after = sent(low_rows, ("gx",), sizes, {"gx": -1})
        before = sent(high_rows, ("gx",), sizes, {"gx": 1})
        field = turned_field(held)
        low, high = columns(field, before, after)
        south = sent(high, ("gy",), sizes, {"gy": 1})
        north = sent(low, ("gy",), sizes, {"gy": -1})
        v1, v2, *kept = fine_part(place, field, before, after)
        strips = strip_part(place, low, high, south, north)
        halves_2 = halves_part(v2, strips, 3)
        halves_0 = lax.ppermute(halves_2, ("tz", "ty"), [(i, i + 1) for i in range(15)])
        sources = sources_part(place, field, strips, v2, *kept)
        source = lax.all_to_all(sources, group_axes, 0, 0)
        to_right, to_left = pack(source)
        source_left = beside(to_right, 1)
        source_right = beside(to_left, -1)
        halves_1 = halves_part(v1, strips, 2)
        starts = ()
        for turn in range(4):
            own = stage(place, starts, (source, source_left, source_right), turn == 3)
            if turn < 3:
                own = sent(own, ("tz",), sizes, {"tz": 1})
                starts = (own, beside(own, 1), beside(own, -1))
            if turn == 2:
                starts, halves_0 = lax.optimization_barrier((starts, halves_0))
        coarse = lax.all_to_all(own, group_axes, 0, 0)
        out = finish(place, tiles, coarse, halves_0, halves_1, halves_2)
        return out.transpose(0, 2, 1, 3).reshape(1, 3, 3, 16, 16, 256)

    spec = P(("tz", "ty"), None, None, None, "gx", "gy")

    return jax.shard_map(per_device, mesh=fine_mesh, in_specs=(spec,), out_specs=spec, check_vma=False)
```

```python
import functools

import jax
import jax.numpy as jnp
from jax import lax
from jax.experimental import pallas as pl
from jax.experimental.pallas import tpu as pltpu
from jax.sharding import Mesh
from jax.sharding import PartitionSpec as P


viscosity = 0.1
slice_step = 0.25
half_step = 0.125
first_row = (5.0 / 24.0, 1.0 / 3.0, -1.0 / 24.0)
second_row = (-1.0 / 24.0, 1.0 / 3.0, 5.0 / 24.0)

f32 = jnp.float32
group_axes = ("ty", "gx")


def snake(piece):
    return piece if piece // 4 % 2 == 0 else piece // 4 * 4 + 3 - piece % 4


def device_of(piece, gy):
    return jnp.where(gy % 2 == 0, snake(piece), snake(15 - piece))


def near(*arrays):
    return tuple(pltpu.with_memory_space_constraint(a, pltpu.VMEM) for a in arrays)


def lanes(shape):
    return lax.broadcasted_iota(jnp.int32, shape, len(shape) - 1)


def strided(u, k, x, half):
    at = k * 512 + x // 8 * 16 + half * 8 + x % 8
    return jnp.concatenate([u[pl.ds(at + 32 * odd, 8, stride=64), :] for odd in (0, 1)], axis=0)


def edges_body(u, held, low_rows, high_rows, arrived):
    copies = [
        pltpu.make_async_copy(u.at[pl.ds(512 * k, 512)], held.at[pl.ds(512 * k, 512)], arrived.at[k])
        for k in range(9)
    ]
    for copy in copies:
        copy.start()
    for k in range(9):
        copies[k].wait()
        for x in (0, 1, 2, 13, 14, 15):
            to = low_rows.at[k, x] if x < 3 else high_rows.at[k, x - 13]
            for half in range(2):
                to[:, half * 128:(half + 1) * 128] = strided(held, k, x, half)


def edges(u):
    vmem = pl.BlockSpec(memory_space=pltpu.VMEM)
    rows = pltpu.VMEM((9, 3, 16, 256), f32)
    return pl.pallas_call(
        edges_body,
        in_specs=[pl.BlockSpec(memory_space=pltpu.HBM)],
        out_specs=[vmem] * 3,
        out_shape=(pltpu.VMEM((4608, 128), f32), rows, rows),
        scratch_shapes=[pltpu.SemaphoreType.DMA((9,))],
        compiler_params=pltpu.CompilerParams(vmem_limit_bytes=12 * 2**20),
        name="edges",
    )(pltpu.with_memory_space_constraint(u, pltpu.HBM))


def turned_body(held, field):
    def each(k, carry):
        for x in range(16):
            for half in range(2):
                field[k, x, :, half * 128:(half + 1) * 128] = strided(held, k, x, half)
        return carry

    lax.fori_loop(0, 9, each, 0)


def turned_field(held):
    vmem = pl.BlockSpec(memory_space=pltpu.VMEM)
    return pl.pallas_call(
        turned_body,
        in_specs=[vmem],
        out_specs=vmem,
        out_shape=pltpu.VMEM((9, 16, 16, 256), f32),
        compiler_params=pltpu.CompilerParams(vmem_limit_bytes=8 * 2**20),
        name="turned",
    )(*near(held))


def columns_body(field, before, after, low, high):
    lane = lanes((16, 128))

    def each(k, carry):
        for t in range(3):
            one = jnp.zeros((16, 128), f32)
            two = jnp.zeros((16, 128), f32)
            for e in range(8 * t, min(8 * t + 8, 22)):
                ref, x = (before, e) if e < 3 else (field, e - 3) if e < 19 else (after, e - 19)
                at = e % 8 * 16
                turned_one = pltpu.roll(ref[k, x, :, 0:128], at + 4, 1)
                turned_two = pltpu.roll(ref[k, x, :, 128:256], (at + 12) % 128, 1)
                one = jnp.where((lane >= at + 4) & (lane < at + 16), turned_one, one)
                two = jnp.where((lane >= at) & (lane < at + 12), turned_two, two)
            low[k, :, t * 128:(t + 1) * 128] = one
            high[k, :, t * 128:(t + 1) * 128] = two
        return carry

    lax.fori_loop(0, 9, each, 0)


def columns(field, before, after):
    vmem = pl.BlockSpec(memory_space=pltpu.VMEM)
    shape = pltpu.VMEM((9, 16, 384), f32)
    return pl.pallas_call(
        columns_body,
        in_specs=[vmem] * 3,
        out_specs=[vmem] * 2,
        out_shape=(shape, shape),
        compiler_params=pltpu.CompilerParams(vmem_limit_bytes=3 * 2**20),
        name="columns",
    )(*near(field, before, after))


def tendency(below, row, above, reach, spacing):
    width = row[0].shape[-1]
    square = 1.0 / (spacing * spacing)
    out = []
    for c in range(3):
        u = row[c]
        up = jnp.concatenate([u[8:16], pltpu.roll(u[0:8], 7, 0)], axis=0)
        down = jnp.concatenate([pltpu.roll(u[8:16], 1, 0), u[0:8]], axis=0)
        north = pltpu.roll(u, width - reach, 1)
        south = pltpu.roll(u, reach, 1)
        laplace = (above[c] + below[c]) + (up + down) - (4.0 + 2.0 * square) * u
        laplace = laplace + (north + south) * square
        transport = (
            row[0] * (above[c] - below[c])
            + row[1] * ((north - south) * (1.0 / spacing))
            + row[2] * (up - down)
        )
        out.append((2.0 * viscosity) * laplace - transport)
    return out


quarter = 0.5 * slice_step
one_0, one_1, one_2 = (quarter * w for w in first_row)
two_0, two_1, two_2 = (quarter * w for w in second_row)


def put(natives, base, x, value):
    for odd in (0, 1):
        at = pl.ds(base + x % 2 * 128 + x // 2 + odd * 8, 8, stride=16)
        for half, native in enumerate(natives):
            native[at, :] = value[odd * 8:odd * 8 + 8, half * 128:(half + 1) * 128]


def split_pairs(native, start, scratch):
    scratch[...] = native[pl.ds(start, 128), :].T
    return scratch[pl.ds(0, 64, stride=2), :], scratch[pl.ds(1, 64, stride=2), :]


def edge_factor(place, axis, low):
    return jnp.where(place[axis] > 0 if low else place[axis] < 3, 1.0, 0.0).astype(f32)


def paired(field):
    width = field.shape[-1]
    even = lanes(field.shape) % 2 == 0
    return 0.5 * (field + jnp.where(even, pltpu.roll(field, width - 1, 1), pltpu.roll(field, 1, 1)))


def swept(rows_of):
    flux = [tendency(*rows_of(node), 1, 1.0) for node in range(3)]
    start = rows_of(0)[1]
    new = [start[c] + (one_0 * flux[0][c] + one_1 * flux[1][c] + one_2 * flux[2][c]) for c in range(3)]
    rest = [two_0 * flux[0][c] + (two_1 - 0.5 * half_step) * flux[1][c] + two_2 * flux[2][c] for c in range(3)]
    return new, rest, flux[0]


def source_pair(leader, start, a, b, d, base_u, base_v):
    one = one_0 * a + one_1 * b + one_2 * d
    two = two_0 * a + two_1 * b + two_2 * d
    one = one + jnp.where(leader, start, (-0.5 * half_step) * base_u)
    return one, two - (0.5 * half_step) * base_v


def first_sweep(rows_of, factor, at, v1, rest, f0):
    new, more, flux = swept(rows_of)
    for c in range(3):
        value = new[c] if factor is None else new[c] * factor
        v1[c, at] = value
        rest[c, at] = more[c]
        f0[c, at] = flux[c]


def inner_body(field, *outs):
    def first(e, carry):
        first_sweep(
            lambda node: [[field[3 * node + c, e - 3 + d] for c in range(3)] for d in (-1, 0, 1)], None, e - 4, *outs
        )
        return carry

    lax.fori_loop(4, 18, first, 0)


def inner_part(field):
    vmem = pl.BlockSpec(memory_space=pltpu.VMEM)
    return pl.pallas_call(
        inner_body,
        out_shape=[pltpu.VMEM((3, 14, 16, 256), f32)] * 3,
        in_specs=[vmem],
        out_specs=[vmem] * 3,
        compiler_params=pltpu.CompilerParams(vmem_limit_bytes=3 * 2**20),
        name="inner",
    )(*near(field))


def fine_body(place, field, before, after, *rest_of):
    inner = rest_of[:3]
    v1, f0, pair_u, pair_v, v2, h1, rest, ue, arrived = rest_of[3:]
    low_ok = edge_factor(place, 0, True)
    high_ok = edge_factor(place, 0, False)

    copies = [
        pltpu.make_async_copy(source, to.at[:, pl.ds(4, 14)], arrived.at[i])
        for i, (source, to) in enumerate(zip(inner, (v1, rest, f0)))
    ]
    for copy in copies:
        copy.start()

    def gather(k, carry):
        for e in (0, 1, 2, 3, 4, 17, 18, 19, 20, 21):
            ref, x = (before, e) if e < 3 else (field, e - 3) if e < 19 else (after, e - 19)
            ue[k, e] = ref[k, x]
        return carry

    lax.fori_loop(0, 9, gather, 0)
    for copy in copies:
        copy.wait()

    def row_ok(e):
        return jnp.where(e < 3, low_ok, jnp.where(e > 18, high_ok, 1.0))

    def first(i, carry):
        e = jnp.where(i < 3, i + 1, i + 15)
        first_sweep(
            lambda node: [[ue[3 * node + c, e + d] for c in range(3)] for d in (-1, 0, 1)],
            row_ok(e), e, v1, rest, f0,
        )
        return carry

    lax.fori_loop(0, 6, first, 0)

    def pairs_of(e, carry):
        for c in range(3):
            pair_v[c, e] = paired(v1[c, e])
        return carry

    lax.fori_loop(2, 20, pairs_of, 0)
    for e in range(2, 20):
        for c in range(3):
            ref, x = (before, e) if e < 3 else (field, e - 3) if e < 19 else (after, e - 19)
            pair_u[c, e] = paired(ref[c, x])

    def second(e, carry):
        rows = [[v1[c, e + d] for c in range(3)] for d in (-1, 0, 1)]
        slope = tendency(*rows, 1, 1.0)
        for c in range(3):
            v2[c, e] = (rows[1][c] + (0.5 * half_step) * slope[c] + rest[c, e]) * row_ok(e)
            h1[c, e] = slope[c]
        return carry

    lax.fori_loop(2, 20, second, 0)


def fine_part(place, field, before, after, inner):
    vmem = pl.BlockSpec(memory_space=pltpu.VMEM)
    return pl.pallas_call(
        fine_body,
        out_shape=[pltpu.VMEM((3, 22, 16, 256), f32)] * 6,
        in_specs=[pl.BlockSpec(memory_space=pltpu.SMEM)] + [vmem] * 3 + [pl.BlockSpec(memory_space=pltpu.HBM)] * 3,
        out_specs=[vmem] * 6,
        scratch_shapes=[
            pltpu.VMEM((3, 22, 16, 256), f32),
            pltpu.VMEM((9, 22, 16, 256), f32),
            pltpu.SemaphoreType.DMA((3,)),
        ],
        compiler_params=pltpu.CompilerParams(vmem_limit_bytes=8 * 2**20),
        name="fine",
    )(place, *near(field, before, after), *(pltpu.with_memory_space_constraint(a, pltpu.HBM) for a in inner))


def strip_body(place, low, high, south, north, strips):
    lane = lanes((16, 768))
    row = lane % 384 // 16
    south_side = (lane < 384) & (lane % 16 < 4)
    north_side = (lane >= 384) & (lane % 16 > 11)
    column_ok = jnp.where(south_side, edge_factor(place, 1, True), jnp.where(north_side, edge_factor(place, 1, False), 1.0))
    rows_ok = jnp.where(row < 3, edge_factor(place, 0, True), jnp.where(row > 18, edge_factor(place, 0, False), 1.0))
    ok = column_ok * rows_ok
    slot = lanes((16, 384)) % 16

    def whole(k):
        left = jnp.where(slot < 4, pltpu.roll(south[k], 376, 1), low[k])
        right = jnp.where(slot > 11, pltpu.roll(north[k], 8, 1), high[k])
        return jnp.concatenate([left, right], axis=1)

    def around(rows):
        return [pltpu.roll(r, 16, 1) for r in rows], rows, [pltpu.roll(r, 752, 1) for r in rows]

    u = [[whole(3 * node + c) for c in range(3)] for node in range(3)]
    nodes = [around(u[node]) for node in range(3)]
    new, more, flux = swept(lambda node: nodes[node])
    v1 = [value * ok for value in new]
    h1 = tendency(*around(v1), 1, 1.0)
    v2 = [(v1[c] + (0.5 * half_step) * h1[c] + more[c]) * ok for c in range(3)]
    h2 = tendency(*around(v2), 1, 1.0)
    base_u = tendency(*around([paired(x) for x in u[0]]), 2, 2.0)
    base_v = tendency(*around([paired(x) for x in v1]), 2, 2.0)
    for c in range(3):
        one, two = source_pair(place[2] == 0, u[0][c], flux[c], h1[c], h2[c], base_u[c], base_v[c])
        for part, value in enumerate((one, two, v1[c], v2[c])):
            for t in range(6):
                strips[part * 3 + c, t] = value[:, t * 128:(t + 1) * 128]


def strip_part(place, *arrays):
    vmem = pl.BlockSpec(memory_space=pltpu.VMEM)
    return pl.pallas_call(
        strip_body,
        out_shape=pltpu.VMEM((12, 6, 16, 128), f32),
        in_specs=[pl.BlockSpec(memory_space=pltpu.SMEM)] + [vmem] * 4,
        out_specs=vmem,
        compiler_params=pltpu.CompilerParams(vmem_limit_bytes=8 * 2**20),
        name="strip",
    )(place, *near(*arrays))


def joined(value, strips, at, e):
    lane = lanes((16, 128))
    shift = e % 8 * 16
    left = pltpu.roll(strips[at, e // 8], 124 - shift, 1)
    right = pltpu.roll(strips[at, 3 + e // 8], 116 - shift, 1)
    low = jnp.where(lane < 4, left, value[:, 0:128])
    high = jnp.where(lane >= 124, right, value[:, 128:256])
    return jnp.concatenate([low, high], axis=1)


def halves_body(values, strips, halves, native_0, native_1, turned, part):
    def moved(e, carry):
        for c in range(3):
            put((native_0, native_1), c * 256, e - 3, joined(values[c, e], strips, part * 3 + c, e))
        return carry

    lax.fori_loop(3, 19, moved, 0)

    for c in range(3):
        for odd in (0, 1):
            tile = c * 256 + odd * 128
            for half, native in enumerate((native_0, native_1)):
                one, two = split_pairs(native, tile, turned.at[(c * 2 + odd) * 2 + half])
                halves[half * 64:half * 64 + 64, tile:tile + 128] = 0.5 * (one - two)


def halves_part(values, strips, part):
    vmem = pl.BlockSpec(memory_space=pltpu.VMEM)
    return pl.pallas_call(
        functools.partial(halves_body, part=part),
        out_shape=pltpu.VMEM((128, 768), f32),
        in_specs=[vmem] * 2,
        out_specs=vmem,
        scratch_shapes=[pltpu.VMEM((768, 128), f32)] * 2 + [pltpu.VMEM((12, 128, 128), f32)],
        compiler_params=pltpu.CompilerParams(vmem_limit_bytes=8 * 2**20),
        name="halves",
    )(*near(values, strips))


def sources_body(place, field, strips, v2, f0, h1, pair_u, pair_v, sources, native_0, native_1, turned):
    gy = place[1]
    leader = place[2] == 0
    natives = (native_0, native_1)

    def third(e, carry):
        slope = tendency(*[[v2[c, e + d] for c in range(3)] for d in (-1, 0, 1)], 1, 1.0)
        base_u = tendency(*[[pair_u[c, e + d] for c in range(3)] for d in (-1, 0, 1)], 2, 2.0)
        base_v = tendency(*[[pair_v[c, e + d] for c in range(3)] for d in (-1, 0, 1)], 2, 2.0)
        for c in range(3):
            both = source_pair(leader, field[c, e - 3], f0[c, e], h1[c, e], slope[c], base_u[c], base_v[c])
            for part, value in enumerate(both):
                put(natives, (3 * part + c) * 256, e - 3, joined(value, strips, 3 * part + c, e))
        return carry

    lax.fori_loop(3, 19, third, 0)

    def compact(c, carry):
        for part in range(2):
            for odd in (0, 1):
                start = pl.multiple_of((part * 3 + c) * 256 + odd * 128, 128)
                for half, native in enumerate(natives):
                    one, two = split_pairs(native, start, turned.at[(part * 2 + odd) * 2 + half])
                    mean = 0.5 * (one + two)
                    tile = pl.multiple_of(part * 768 + c * 256 + odd * 128, 128)
                    for i in range(8):
                        sources[device_of(half * 8 + i, gy), :, pl.ds(tile, 128)] = mean[8 * i:8 * i + 8]
        return carry

    lax.fori_loop(0, 3, compact, 0)


def sources_part(place, *arrays):
    vmem = pl.BlockSpec(memory_space=pltpu.VMEM)
    return pl.pallas_call(
        sources_body,
        out_shape=pltpu.VMEM((16, 8, 1536), f32),
        in_specs=[pl.BlockSpec(memory_space=pltpu.SMEM)] + [vmem] * len(arrays),
        out_specs=vmem,
        scratch_shapes=[pltpu.VMEM((1536, 128), f32)] * 2 + [pltpu.VMEM((8, 128, 128), f32)],
        compiler_params=pltpu.CompilerParams(vmem_limit_bytes=16 * 2**20),
        name="sources",
    )(place, *near(*arrays))


def pack_body(source, to_right, to_left):
    row = lax.broadcasted_iota(jnp.int32, (8, 768), 0)
    for j in range(2):
        for field in range(2):
            k = 2 * j + field
            for xh in range(4):
                one = source[j * 4 + xh, :, field * 768:(field + 1) * 768]
                two = source[(3 - j) * 4 + xh, :, (1 - field) * 768:(2 - field) * 768]
                right = pltpu.roll(two, k, 0) if k else two
                left = pltpu.roll(two, 8 - k, 0) if k else two
                to_right[j * 4 + xh, :, field * 768:(field + 1) * 768] = jnp.where(row > k, one, right)
                to_left[j * 4 + xh, :, field * 768:(field + 1) * 768] = jnp.where(row < 7 - k, one, left)


def pack(source):
    vmem = pl.BlockSpec(memory_space=pltpu.VMEM)
    shape = pltpu.VMEM((8, 8, 1536), f32)
    return pl.pallas_call(
        pack_body,
        in_specs=[vmem],
        out_specs=[vmem] * 2,
        out_shape=(shape, shape),
        compiler_params=pltpu.CompilerParams(vmem_limit_bytes=8 * 2**20),
        name="pack",
    )(*near(source))


def stage_body(place, *rest, begins, ends):
    rest = list(rest)
    starts = () if begins else (rest.pop(0), rest.pop(0), rest.pop(0))
    source, source_left, source_right, result, buffer_0, buffer_1 = rest
    lane = lanes((24, 128))
    x_first = lane % 8 == 0
    x_last = lane % 8 == 7
    row = lax.broadcasted_iota(jnp.int32, (24, 128), 0)
    inside = ((row >= 8) | (place[3] > 0)) & ((row < 16) | (place[3] < 63))

    for c in range(3):
        for t in range(8):
            for buffer in (buffer_0, buffer_1):
                buffer[c, t, 0:8] = jnp.zeros((8, 128), f32)
                buffer[c, t, 32:40] = jnp.zeros((8, 128), f32)
            if begins:
                buffer_0[c, t, 8:32] = jnp.zeros((24, 128), f32)
            else:
                own, left, right = starts
                buffer_0[c, t, 8:16] = left[c, t]
                buffer_0[c, t, 16:24] = own[c, t]
                buffer_0[c, t, 24:32] = right[c, t]

    def keep(j, field, buffer):
        for xh in range(4):
            for c in range(3):
                for odd in range(2):
                    at = (field * 6 + c * 2 + odd) * 128
                    result[j * 4 + xh, :, at:at + 128] = buffer[c, xh * 2 + odd, 16:24]

    square = 0.25
    c_side = half_step * viscosity
    c_second = half_step * viscosity * square
    c_centre = 1.0 - half_step * viscosity * (4.0 + 2.0 * square)

    def step(j, field, old, new, late):
        k = 2 * j + field
        for xh in range(4):
            for odd in range(2):
                t = 2 * xh + odd
                u = [old[c, t, 8:32] for c in range(3)]
                k0 = u[0] * (-0.5 * half_step)
                k1 = u[1] * (-0.25 * half_step)
                k2 = u[2] * (-0.5 * half_step)
                for c in range(3):
                    v = u[c]
                    other = old[c, t + 1 - 2 * odd, 8:32]
                    if odd:
                        beyond = pltpu.roll(old[c, t + 1, 8:32], 7, 1) if xh < 3 else 0.0
                        east = jnp.where(x_last, beyond, pltpu.roll(other, 127, 1))
                        west = other
                    else:
                        beyond = pltpu.roll(old[c, t - 1, 8:32], 121, 1) if xh > 0 else 0.0
                        east = other
                        west = jnp.where(x_first, beyond, pltpu.roll(other, 1, 1))
                    up = pltpu.roll(v, 120, 1)
                    down = pltpu.roll(v, 8, 1)
                    north = old[c, t, 9:33]
                    south = old[c, t, 7:31]
                    at = (field * 6 + c * 2 + odd) * 128
                    if late:
                        there = ((1 - field) * 6 + c * 2 + odd) * 128
                        pull_left = pltpu.roll(source_left[(3 - j) * 4 + xh, :, there:there + 128], (1 + k) % 8, 0)
                        pull_right = pltpu.roll(source_right[(3 - j) * 4 + xh, :, there:there + 128], 7 - k, 0)
                    else:
                        pull_left = source_left[j * 4 + xh, :, at:at + 128]
                        pull_right = source_right[j * 4 + xh, :, at:at + 128]
                    pull = jnp.concatenate(
                        [pull_left, source[j * 4 + xh, :, at:at + 128], pull_right], axis=0
                    )
                    value = (
                        c_centre * v
                        + c_side * ((east + west) + (up + down))
                        + c_second * (north + south)
                        + (k0 * (east - west) + k1 * (north - south) + k2 * (up - down))
                        + pull
                    )
                    new[c, t, 8:32] = jnp.where(inside, value, 0.0)

    def one_slice(j, late):
        if ends:
            keep(j, 0, buffer_0)
        step(j, 0, buffer_0, buffer_1, late)
        if ends:
            keep(j, 1, buffer_1)
        step(j, 1, buffer_1, buffer_0, late)
        if ends:
            keep(j, 2, buffer_0)

    def early(j, carry):
        one_slice(j, False)
        return carry

    def later(j, carry):
        one_slice(j, True)
        return carry

    lax.fori_loop(0, 2, early, 0)
    lax.fori_loop(2, 4, later, 0)
    if not ends:
        for c in range(3):
            for t in range(8):
                result[c, t] = buffer_0[c, t, 16:24]


def stage(place, starts, sources, ends):
    vmem = pl.BlockSpec(memory_space=pltpu.VMEM)
    arrays = near(*starts, *sources)
    return pl.pallas_call(
        functools.partial(stage_body, begins=not starts, ends=ends),
        out_shape=pltpu.VMEM((16, 8, 2304) if ends else (3, 8, 8, 128), f32),
        in_specs=[pl.BlockSpec(memory_space=pltpu.SMEM)] + [vmem] * len(arrays),
        out_specs=vmem,
        scratch_shapes=[pltpu.VMEM((3, 8, 40, 128), f32)] * 2,
        compiler_params=pltpu.CompilerParams(vmem_limit_bytes=12 * 2**20),
        name="stage",
    )(place, *arrays)


def finish_body(place, start, coarse, halves_0, halves_1, halves_2, out, mixed, rows):
    gy = place[1]

    def one_field(field, halves):
        for c in range(3):
            for half in range(2):
                for odd in range(2):
                    tile = pl.ds(field * 768 + c * 256 + odd * 128, 128)
                    w = jnp.concatenate(
                        [coarse[device_of(half * 8 + i, gy), :, tile] for i in range(8)], axis=0
                    )
                    e = halves[pl.ds(half * 64, 64), pl.ds(c * 256 + odd * 128, 128)]
                    at = (c * 2 + half) * 2 + odd
                    mixed[at, pl.ds(0, 64, stride=2), :] = w + e
                    mixed[at, pl.ds(1, 64, stride=2), :] = w - e
                    rows[c * 2 + half, pl.ds(odd, 128, stride=2), :] = mixed[at].T
                out[pl.ds(c * 32, 32), half] = rows[c * 2 + half].reshape(32, 8, 128)

    for field, halves in enumerate((halves_0, halves_1, halves_2)):
        if field:
            chosen = pl.program_id(0) == field
        else:
            chosen = (pl.program_id(0) == 0) & (place[2] > 0)
        pl.when(chosen)(functools.partial(one_field, field, halves))

    @pl.when((pl.program_id(0) == 0) & (place[2] == 0))
    def _():
        pltpu.sync_copy(start.at[pl.ds(0, 96)], out)


def finish(place, start, coarse, *halves):
    vmem = pl.BlockSpec(memory_space=pltpu.VMEM)
    return pl.pallas_call(
        finish_body,
        grid=(3,),
        out_shape=jax.ShapeDtypeStruct((288, 2, 8, 128), f32),
        in_specs=[pl.BlockSpec(memory_space=pltpu.SMEM), pl.BlockSpec(memory_space=pl.ANY)] + [vmem] * 4,
        out_specs=pl.BlockSpec((96, 2, 8, 128), lambda f: (f, 0, 0, 0)),
        scratch_shapes=[pltpu.VMEM((12, 128, 128), f32), pltpu.VMEM((6, 256, 128), f32)],
        compiler_params=pltpu.CompilerParams(vmem_limit_bytes=16 * 2**20),
        name="finish",
    )(place, start, *near(coarse), *halves)


def sent(block, axes, sizes, moves):
    strides = {}
    total = 1
    for axis in reversed(axes):
        strides[axis] = total
        total *= sizes[axis]
    pairs = []
    for source in range(total):
        target = source
        for axis, by in moves.items():
            at = source // strides[axis] % sizes[axis]
            if not 0 <= at + by < sizes[axis]:
                target = None
                break
            target += by * strides[axis]
        if target is not None:
            pairs.append((source, target))
    return lax.ppermute(block, axes if len(axes) > 1 else axes[0], pairs)


def solution(mesh):
    sizes = {"tz": 4, "ty": 4, "gx": 4, "gy": 4}
    fine_mesh = Mesh(mesh.devices.reshape(4, 4, 4, 4), tuple(sizes))
    pieces = ("ty", "gx", "gy")

    def beside(block, by):
        def name(piece):
            gy, at = divmod(piece, 16)
            return snake(15 - at if gy % 2 else at) * 4 + gy

        pairs = [(name(i), name(i + by)) for i in range(64) if 0 <= i + by < 64]
        return lax.ppermute(block, pieces, pairs)

    def per_device(provisional):
        tz, ty, gx, gy = (lax.axis_index(a) for a in sizes)
        piece = ty * 4 + jnp.where(ty % 2 == 0, gx, 3 - gx)
        piece = gy * 16 + jnp.where(gy % 2 == 0, piece, 15 - piece)
        place = jnp.stack([gx, gy, tz * 4 + ty, piece]).astype(jnp.int32)
        tiles = provisional.reshape(288, 8, 2, 128).transpose(0, 2, 1, 3)
        held, low_rows, high_rows = edges(tiles.reshape(4608, 128))
        after = sent(low_rows, ("gx",), sizes, {"gx": -1})
        before = sent(high_rows, ("gx",), sizes, {"gx": 1})
        field = turned_field(held)
        inner = inner_part(field)
        low, high = columns(field, before, after)
        south = sent(high, ("gy",), sizes, {"gy": 1})
        north = sent(low, ("gy",), sizes, {"gy": -1})
        v1, f0, pair_u, pair_v, v2, h1 = fine_part(place, field, before, after, inner)
        strips = strip_part(place, low, high, south, north)
        halves_2 = halves_part(v2, strips, 3)
        halves_0 = lax.ppermute(halves_2, ("tz", "ty"), [(i, i + 1) for i in range(15)])
        sources = sources_part(place, field, strips, v2, f0, h1, pair_u, pair_v)
        source = lax.all_to_all(sources, group_axes, 0, 0)
        to_right, to_left = pack(source)
        source_left = beside(to_right, 1)
        source_right = beside(to_left, -1)
        halves_1 = halves_part(v1, strips, 2)
        starts = ()
        for turn in range(4):
            own = stage(place, starts, (source, source_left, source_right), turn == 3)
            if turn < 3:
                own = sent(own, ("tz",), sizes, {"tz": 1})
                starts = (own, beside(own, 1), beside(own, -1))
            if turn == 2:
                starts, halves_0 = lax.optimization_barrier((starts, halves_0))
        coarse = lax.all_to_all(own, group_axes, 0, 0)
        out = finish(place, tiles, coarse, halves_0, halves_1, halves_2)
        return out.transpose(0, 2, 1, 3).reshape(1, 3, 3, 16, 16, 256)

    spec = P(("tz", "ty"), None, None, None, "gx", "gy")

    return jax.shard_map(per_device, mesh=fine_mesh, in_specs=(spec,), out_specs=spec, check_vma=False)
```
